32 devices in a mesh: cuts: 2 (over x), outer: 16 (over z, y, core).
Axes of the slice: x: 2, y: 2, z: 4, core: 2. Of those that a mesh axis runs over, the one named last changes fastest.
Arguments:
- stem_tensor: bfloat16 [32, 512, 2, 512], P(('cuts', 'outer')), parts along dimension 0, may hold values from -6 to 6
- leaf_left: bfloat16 [4, 2, 8192, 2, 512], P(None, None, 'outer'), may hold values from -0.09375 to 0.09375
- leaf_right: bfloat16 [4, 2, 8192, 2, 512], P(None, None, 'outer'), may hold values from -0.125 to 0.125
- slice_bits: int32 [8], P('cuts'), parts along dimension 0, may hold values from 0 to 1, as said below
Outputs:
- stem_out: bfloat16 [32, 512, 2, 512], P(('cuts', 'outer')), parts along dimension 0
The draws below stay inside these ranges and needn't reach their ends.
There are 2 independent parts, one for each index of `cuts`. The reference program is written for one: setup_inputs(seed, part) draws one part's arguments, and reference() takes and returns one part's arrays. A program takes and returns all parts, laid end to end along the dimension named above; an argument that names none is the same for every part. Nothing has to cross between parts.
Inputs may be any that keep to these rules, and one draw needn't show every extreme that they name: `slice_bits`: the first entry is the index of the part modulo 2, so neighbouring parts contract different slices; the other entries are drawn independently.
All inputs are finite; a program needn't handle non-finite values.
Results may differ from the reference program's by a relative error of at most 0.01.
Values may be sent and summed in bfloat16 or wider, within the bound.
A program may use at most 64 MiB of HBM per device.

```python
import jax
import jax.numpy as jnp
from jax import lax

W = 512
K = 8192
ROUNDS = 2
SLICES = 2
BR = 4
SHARDS = 16


def draw_slice_bits(key, part):
    drawn = jax.random.randint(key, (BR,), 0, 2, dtype=jnp.int32)
    first = jnp.asarray(part, jnp.int32) % 2
    return drawn.at[0].set(first)


def with_spikes(entries, own_key, source, target, blocks, factor):
    def block_of(axis_at):
        return (jnp.arange(entries.shape[axis_at]) // (entries.shape[axis_at] // blocks)).reshape((-1,) + (1,) * (entries.ndim - 1 - axis_at))

    one_side = jax.random.permutation(own_key, blocks)[block_of(target)]
    other_side = (block_of(target) + blocks // 2) % blocks
    return jnp.where((block_of(source) == one_side) | (block_of(source) == other_side), factor * entries, entries)


def levels(key, dims, pieces, low, largest):
    gain, own = 1.0, jax.random.fold_in(key, 6)
    for dim, blocks in pieces:
        steps = jnp.exp(jax.random.uniform(jax.random.fold_in(own, dim), (blocks,), jnp.float32, low / len(pieces), largest / len(pieces)))
        gain = gain * jnp.repeat(steps, dims[dim] // blocks).reshape([-1 if axis == dim else 1 for axis in range(len(dims))])
    return gain


def gaussian(stream_key, extent, scale, reach, cuts=(), kind=jnp.bfloat16):
    values = scale * jax.random.normal(stream_key, extent, jnp.float32)
    if cuts:
        values = values * levels(stream_key, extent, cuts, -0.22, 0.18)
    return jnp.clip(values, -reach, reach).astype(kind)


def bell_draw_with(own_key, shape, width, most, cuts, heavy, kind=jnp.bfloat16):
    values = width * jax.random.normal(own_key, shape, jnp.float32)
    if cuts:
        values = values * levels(own_key, shape, cuts, -0.22, 0.18)
    return jnp.clip(with_spikes(values, jax.random.fold_in(own_key, 3), *heavy), -most, most).astype(kind)


def setup_inputs(seed: int = 0, part: int = 0) -> dict:
    keys = jax.random.split(jax.random.key(seed), 5)
    part_splits = jax.random.split(jax.random.fold_in(keys[4], part), 5)
    stem_tensor = gaussian(part_splits[0], (SHARDS, W, 2, W), 1.0, 6.0, ((0, 16),))
    leaf_left = bell_draw_with(keys[1], (BR, SLICES, K, 2, W), K ** -0.5, 0.09375, ((2, 16),), (2, 4, 16, 2.0))
    leaf_right = gaussian(keys[2], (BR, SLICES, K, 2, W), (4 * W) ** -0.5, 0.125, ((2, 16),))
    slice_bits = draw_slice_bits(jax.random.fold_in(jax.random.fold_in(keys[4], part), 71), part)
    return {"stem_tensor": stem_tensor, "leaf_left": leaf_left, "leaf_right": leaf_right, "slice_bits": slice_bits}


def complex_leaves(left_leaf, right_leaf):
    product = jnp.einsum('kpi,kqm->piqm', left_leaf, right_leaf)
    real_part = product[0, :, 0] - product[1, :, 1]
    imag_part = product[0, :, 1] + product[1, :, 0]
    return jnp.stack([real_part, imag_part], axis=1)


def reference(stem_tensor, leaf_left, leaf_right, slice_bits):
    branches = []
    for branch_index in range(2 * ROUNDS):
        chosen = slice_bits[branch_index].astype(jnp.int32)
        left_leaf = lax.dynamic_index_in_dim(leaf_left[branch_index], chosen, 0, keepdims=False).astype(jnp.float32)
        right_leaf = lax.dynamic_index_in_dim(leaf_right[branch_index], chosen, 0, keepdims=False).astype(jnp.float32)
        branches.append(complex_leaves(left_leaf, right_leaf).astype(jnp.bfloat16))
    shards = SHARDS
    span = W // SHARDS
    state = stem_tensor
    for round_index in range(ROUNDS):
        p_branch = branches[2 * round_index].astype(jnp.float32)
        q_branch = branches[2 * round_index + 1].astype(jnp.float32)
        current = state.astype(jnp.float32)
        product = jnp.einsum('abpc,cqm->abpqm', current, q_branch)
        real_part = product[:, :, 0, 0] - product[:, :, 1, 1]
        imag_part = product[:, :, 0, 1] + product[:, :, 1, 0]
        absorbed = jnp.stack([real_part, imag_part], axis=2).astype(jnp.bfloat16)
        grouped = absorbed.astype(jnp.float32).reshape(shards, shards, span, 2, W)
        p_grouped = p_branch.reshape(shards, span, 2, W)
        product = jnp.einsum('ahlpm,alqn->hnpqm', grouped, p_grouped)
        real_part = product[:, :, 0, 0] - product[:, :, 1, 1]
        imag_part = product[:, :, 0, 1] + product[:, :, 1, 0]
        state = jnp.stack([real_part, imag_part], axis=2).astype(jnp.bfloat16)
    return state
```

```python
import functools

import jax
import jax.numpy as jnp
from jax import lax
from jax.experimental import pallas as pl
from jax.experimental.pallas import tpu as pltpu
from jax.sharding import PartitionSpec as P

MESH = pl.DeviceIdType.MESH
LANES = 128
STAGES = (1.6, 4.5, 3.5, 3.5)
ENTRIES = {0: 5.0, 2: 10.0, 1: 15.0, 3: 20.0}
PLANE_GAP = 0.4
LEAVES = {0: 3.0, 2: 6.0, 1: 9.5, 3: 13.0}
FIRST_SENDS = (2.0, 4.9, 9.0, 14.0)
SPLITS = (15.0, 18.0, 21.0, 24.0)


def network_kernel(
    n, bits, stem, left, right, out,
    l0, l1, l2, l3, r0, r1, r2, r3, part, outgoing, incoming, branch, got0, planes, blocks1, got1, absorbed,
    q_product, mixed, wide, leaf_sem, own_sem, a_send, a_recv, r_send, r_recv,
):
    chunks, _, span, columns = part.shape
    width = n * span
    steps = n.bit_length() - 1
    group = n // 4
    me = lax.axis_index("outer")
    lefts, rights = (l0, l1, l2, l3), (r0, r1, r2, r3)

    def flipped(k):
        total = 0
        for s in range(steps):
            both = lax.rem(me // (1 << s), 2) + lax.rem(k // (1 << s), 2)
            total = total + lax.rem(both, 2) * (1 << s)
        return total

    def reversed_bits(k):
        return sum(lax.rem(k // (1 << s), 2) * (n >> (s + 1)) for s in range(steps))

    bit = [lax.rem(me // (1 << s), 2) for s in range(steps)]
    partners = [me + (1 << s) * (1 - 2 * bit[s]) for s in range(steps)]
    starts = [0]
    gives = []
    for s in range(steps):
        half = n >> (s + 1)
        gives.append(starts[s] + (1 - bit[s]) * half)
        starts.append(starts[s] + bit[s] * half)

    barrier = pltpu.get_barrier_semaphore()

    def greet(k, carry):
        pl.semaphore_signal(barrier, inc=1, device_id={"outer": lax.rem(me + k, n)}, device_id_type=MESH)
        return carry

    lax.fori_loop(1, n, greet, 0)

    def leaf_copies(j):
        return (
            pltpu.make_async_copy(left.at[j], lefts[j], leaf_sem.at[j, 0]),
            pltpu.make_async_copy(right.at[j], rights[j], leaf_sem.at[j, 1]),
        )

    def each(first, last, act):
        def one(k, carry):
            act(k)
            return carry

        if last - first <= 4:
            for k in range(first, last):
                act(k)
        else:
            lax.fori_loop(first, last, one, 0)

    def first_copy(k):
        to = flipped(k)
        return pltpu.make_async_remote_copy(
            src_ref=stem.at[to], dst_ref=got0.at[me], send_sem=a_send.at[0, k], recv_sem=a_recv.at[0, k],
            device_id={"outer": to}, device_id_type=MESH)

    def first_arrival(k):
        origin = flipped(k)
        return pltpu.make_async_remote_copy(
            src_ref=stem.at[origin], dst_ref=got0.at[origin], send_sem=a_send.at[0, k], recv_sem=a_recv.at[0, k],
            device_id={"outer": origin}, device_id_type=MESH)

    def second_copy(k):
        to = flipped(k)
        return pltpu.make_async_remote_copy(
            src_ref=blocks1.at[reversed_bits(to)], dst_ref=got1.at[me // 4, lax.rem(me, 4)],
            send_sem=a_send.at[1, k], recv_sem=a_recv.at[1, k],
            device_id={"outer": to}, device_id_type=MESH)

    def second_arrival(k):
        origin = flipped(k)
        return pltpu.make_async_remote_copy(
            src_ref=blocks1.at[reversed_bits(origin)], dst_ref=got1.at[origin // 4, lax.rem(origin, 4)],
            send_sem=a_send.at[1, k], recv_sem=a_recv.at[1, k],
            device_id={"outer": origin}, device_id_type=MESH)

    own_copy = pltpu.make_async_copy(stem.at[me], got0.at[me], own_sem)

    def send_first(i):
        each(group * i if i else 1, group * (i + 1), lambda k: first_copy(k).start())

    def split(i):
        each(group * i if i else 1, group * (i + 1), lambda k: first_arrival(k).wait_recv())
        if i == 0:
            own_copy.wait()
        here = pl.ds(flipped(group * i) // group * group, group)
        rows = group * span
        entries = got0[here].reshape(2 * rows, columns).astype(jnp.float32)
        for t in range(columns // LANES):
            lanes = slice(t * LANES, (t + 1) * LANES)
            wide[t, 0 : 2 * rows] = entries[:, lanes]
            for p in range(2):
                plane = wide[t, pl.ds(p, rows, stride=2), :]
                planes[p, here, :, lanes] = plane.astype(jnp.bfloat16).reshape(group, span, LANES)

    def dot(a, b):
        return jnp.dot(a, b, preferred_element_type=jnp.float32)

    def leaf_product(j):
        for copy in leaf_copies(j):
            copy.wait()
        chosen = bits[j]
        plain_ref, other_ref = (rights[j], lefts[j]) if j % 2 == 0 else (lefts[j], rights[j])
        rows = 2 * plain_ref.shape[1]
        plain = plain_ref[chosen].reshape(rows, plain_ref.shape[3])
        other = other_ref[chosen].reshape(rows, other_ref.shape[3]).astype(jnp.float32)
        even = lax.rem(lax.broadcasted_iota(jnp.int32, other.shape, 0), 2) == 0
        signed = jnp.where(even, other, -other).astype(jnp.bfloat16)
        swapped = jnp.where(even, pltpu.roll(other, rows - 1, 0), pltpu.roll(other, 1, 0)).astype(jnp.bfloat16)
        dims = (((0,), (0,)), ((), ()))
        for p, factor in enumerate((signed, swapped)):
            product = lax.dot_general(plain, factor, dims, preferred_element_type=jnp.float32)
            product = product.reshape(n, span, columns)
            if j == 0:
                for b in range(n):
                    at = sum((b >> s & 1) * (n >> (s + 1)) for s in range(steps))
                    part[p, at] = product[b]
            else:
                part[2 * j + p] = product

    def reduce_copy(c, s):
        half, at = n >> (s + 1), n - (n >> s)
        return pltpu.make_async_remote_copy(
            src_ref=outgoing.at[c, pl.ds(gives[s], half)], dst_ref=incoming.at[c, pl.ds(at, half)],
            send_sem=r_send.at[c, s], recv_sem=r_recv.at[c, s],
            device_id={"outer": partners[s]}, device_id_type=MESH)

    def gather_copy(c, s, first):
        here = branch.at[c, pl.ds(first, n >> (s + 1))]
        return pltpu.make_async_remote_copy(
            src_ref=here, dst_ref=here, send_sem=r_send.at[c, 2 * steps - 1 - s], recv_sem=r_recv.at[c, 2 * steps - 1 - s],
            device_id={"outer": partners[s]}, device_id_type=MESH)

    def begin(c, step):
        if step < steps:
            give = pl.ds(gives[step], n >> (step + 1))
            outgoing[c, give] = part[c, give].astype(outgoing.dtype)
            reduce_copy(c, step).start()
        else:
            s = 2 * steps - 1 - step
            gather_copy(c, s, starts[s + 1]).start()

    def finish(c, step):
        if step < steps:
            half, at = n >> (step + 1), n - (n >> step)
            reduce_copy(c, step).wait_recv()
            keep = pl.ds(starts[step + 1], half)
            total = part[c, keep] + incoming[c, pl.ds(at, half)].astype(jnp.float32)
            if step == steps - 1:
                branch[c, keep] = total.astype(branch.dtype)
            else:
                part[c, keep] = total
        else:
            s = 2 * steps - 1 - step
            gather_copy(c, s, gives[s]).wait_recv()

    def turn(c, step):
        if step:
            finish(c, step - 1)
        if step < 2 * steps:
            begin(c, step)

    def near(low):
        core = lax.rem(bit[0] + low % 2, 2)
        side = lax.rem(bit[1] + low // 2, 2)
        return core, side

    def contract_first(low):
        core, side = near(low)
        here = pl.ds(core * (n // 2) + side * (n // 4), group)
        p_real = branch[0, here].reshape(group * span, width)
        p_imag = branch[1, here].reshape(group * span, width)
        a_real, a_imag = planes[0].reshape(width, columns), planes[1].reshape(width, columns)
        real_part = (dot(p_real, a_real) - dot(p_imag, a_imag)).astype(jnp.bfloat16)
        imag_part = (dot(p_real, a_imag) + dot(p_imag, a_real)).astype(jnp.bfloat16)
        blocks1[here, 0:span] = real_part.reshape(group, span, columns)
        blocks1[here, span : 2 * span] = imag_part.reshape(group, span, columns)
        if low == 0:
            got1[me // 4, lax.rem(me, 4)] = blocks1[starts[steps]]
        if group == 4:
            for q in (2, 3, 1, 0):
                if q or low:
                    second_copy(4 * q + low).start()
        else:
            each(0 if low else 1, group, lambda q: second_copy(4 * q + low).start())

    def interleave():
        for t in range(width // LANES):
            lanes = slice(t * LANES, (t + 1) * LANES)
            p_real, p_imag = (
                branch[4 + p, :, :, lanes].reshape(width, LANES).astype(jnp.float32) for p in range(2))
            for k, (even, odd) in enumerate(((p_real, p_imag), (-p_imag, p_real))):
                wide[t, pl.ds(0, width, stride=2), :] = even
                wide[t, pl.ds(1, width, stride=2), :] = odd
                mixed[k, :, lanes] = wide[t].astype(jnp.bfloat16)

    def multiply():
        a_real, a_imag, b_real, b_imag = (branch[c].reshape(width, columns) for c in (2, 3, 6, 7))
        q_product[0] = (dot(a_real, b_real) - dot(a_imag, b_imag)).astype(jnp.bfloat16)
        q_product[1] = (dot(a_real, b_imag) + dot(a_imag, b_real)).astype(jnp.bfloat16)

    def absorb(low):
        each(0 if low else 1, group, lambda q: second_arrival(4 * q + low).wait_recv())
        core, side = near(low)
        entries = got1[:, core + 2 * side].reshape(group * 2 * span, columns)
        by_real = dot(entries, q_product[0]).reshape(group, 2, span, columns)
        by_imag = dot(entries, q_product[1]).reshape(group, 2, span, columns)
        absorbed[0, :, core + 2 * side] = (by_real[:, 0] - by_imag[:, 1]).astype(absorbed.dtype)
        absorbed[1, :, core + 2 * side] = (by_imag[:, 0] + by_real[:, 1]).astype(absorbed.dtype)

    def contract_last(tile):
        rows = width // 4
        here = pl.ds(2 * rows * tile, 2 * rows)
        a_real, a_imag = absorbed[0].reshape(width, columns), absorbed[1].reshape(width, columns)
        total = dot(mixed[0, here], a_real) + dot(mixed[1, here], a_imag)
        out[rows * tile : rows * (tile + 1)] = total.astype(jnp.bfloat16).reshape(rows, 2, columns)

    for j in (0, 2, 1, 3):
        for copy in leaf_copies(j):
            copy.start()
    own_copy.start()
    pl.semaphore_wait(barrier, n - 1)

    events = []
    for i, time in zip((2, 3, 1, 0), FIRST_SENDS):
        events.append((time, functools.partial(send_first, i)))
    for i, time in zip((2, 3, 1, 0), SPLITS):
        events.append((time, functools.partial(split, i)))
    for j, time in LEAVES.items():
        events.append((time, functools.partial(leaf_product, j)))
    stages = [STAGES[min(s, 3)] for s in range(steps)]
    stages = stages + stages[::-1]
    done = {}
    for j, time in ENTRIES.items():
        for p in range(2):
            for step in range(2 * steps + 1):
                at = time + PLANE_GAP * p + sum(stages[:step])
                events.append((at, functools.partial(turn, 2 * j + p, step)))
                done[j, step] = at
    for low, s in ((0, 2), (2, 1), (1, 0), (3, 0)):
        at = done[0, 2 * steps - s] + 0.01
        assert at > max(SPLITS)
        events.append((at, functools.partial(contract_first, low)))
    end = done[2, 2 * steps] + 0.01
    events.append((end, interleave))
    end = max(done[1, 2 * steps], done[3, 2 * steps]) + 0.01
    events.append((end, multiply))
    end = max(at for at, _ in events)
    for i, low in enumerate((0, 2, 1, 3)):
        events.append((end + i + 1, functools.partial(absorb, low)))
    for tile in range(4):
        events.append((end + tile + 6, functools.partial(contract_last, tile)))
    for _, act in sorted(events, key=lambda event: event[0]):
        act()

    def settle(k, carry):
        first_copy(k).wait_send()
        second_copy(k).wait_send()
        return carry

    lax.fori_loop(1, n, settle, 0)
    for c in range(chunks):
        for s in range(steps):
            reduce_copy(c, s).wait_send()
            gather_copy(c, s, starts[s + 1]).wait_send()


def on_device(n, stem_tensor, leaf_left, leaf_right, slice_bits):
    branches, slices, depth, _, rows = leaf_left.shape
    width, columns = stem_tensor.shape[1], stem_tensor.shape[3]
    span = width // n
    steps = n.bit_length() - 1
    blocks = stem_tensor.reshape(n, span, 2, columns)
    both = (2 * branches, n, span, columns)
    anywhere = pl.BlockSpec(memory_space=pl.ANY)
    state = pl.pallas_call(
        functools.partial(network_kernel, n),
        out_shape=jax.ShapeDtypeStruct((width, 2, columns), jnp.bfloat16),
        in_specs=[pl.BlockSpec(memory_space=pltpu.SMEM), anywhere, anywhere, anywhere],
        out_specs=pl.BlockSpec(memory_space=pltpu.VMEM),
        scratch_shapes=[
            *[pltpu.VMEM((slices, depth, 2, rows), jnp.bfloat16)] * branches,
            *[pltpu.VMEM((slices, depth, 2, columns), jnp.bfloat16)] * branches,
            pltpu.VMEM(both, jnp.float32),
            pltpu.VMEM(both, jnp.bfloat16),
            pltpu.VMEM(both, jnp.bfloat16),
            pltpu.VMEM(both, jnp.bfloat16),
            pltpu.VMEM((n, span, 2, columns), jnp.bfloat16),
            pltpu.VMEM((2, n, span, columns), jnp.bfloat16),
            pltpu.VMEM((n, 2 * span, columns), jnp.bfloat16),
            pltpu.VMEM((n // 4, 4, 2 * span, columns), jnp.bfloat16),
            pltpu.VMEM((2, n // 4, 4, span, columns), jnp.bfloat16),
            pltpu.VMEM((2, width, columns), jnp.bfloat16),
            pltpu.VMEM((2, 2 * width, columns), jnp.bfloat16),
            pltpu.VMEM((columns // LANES, 2 * width, LANES), jnp.float32),
            pltpu.SemaphoreType.DMA((branches, 2)),
            pltpu.SemaphoreType.DMA,
            pltpu.SemaphoreType.DMA((2, n)),
            pltpu.SemaphoreType.DMA((2, n)),
            pltpu.SemaphoreType.DMA((2 * branches, 2 * steps)),
            pltpu.SemaphoreType.DMA((2 * branches, 2 * steps)),
        ],
        compiler_params=pltpu.CompilerParams(
            collective_id=0, has_side_effects=True, vmem_limit_bytes=60 * 1024 * 1024),
    )(slice_bits, blocks, leaf_left, leaf_right)
    return state[None]


def solution(mesh):
    return jax.shard_map(
        functools.partial(on_device, mesh.shape["outer"]),
        mesh=mesh,
        in_specs=(
            P(("cuts", "outer"), None, None, None),
            P(None, None, "outer", None, None),
            P(None, None, "outer", None, None),
            P("cuts"),
        ),
        out_specs=P(("cuts", "outer"), None, None, None),
        check_vma=False,
    )
```

```python
import functools

import jax
import jax.numpy as jnp
from jax import lax
from jax.experimental import pallas as pl
from jax.experimental.pallas import tpu as pltpu
from jax.sharding import PartitionSpec as P

MESH = pl.DeviceIdType.MESH
LANES = 128
TILES = 4
LEAF_ORDER = (2, 3, 1)
PIECES = (2, 1, 2, 1)


def pieces_of(planes, span):
    parts = []
    for plane in range(planes):
        pieces = PIECES[plane // 2] if span % 32 == 0 else 1
        parts += [(plane, pl.ds(h * (span // pieces), span // pieces)) for h in range(pieces)]
    return parts


def schedule(n, steps, parts):
    events = []

    def at(time, *event):
        events.append((time, event))

    TABLE = [
        ('first', 14),
        ('first', 3),
        ('turn', 1, 0),
        ('first', 12),
        ('first', 4),
        ('first', 9),
        ('turn', 3, 0),
        ('first', 2),
        ('leaf', 2),
        ('first', 5),
        ('turn', 6, 0),
        ('turn', 7, 0),
        ('turn', 3, 1),
        ('leaf', 3),
        ('turn', 1, 1),
        ('turn', 0, 0),
        ('turn', 7, 1),
        ('turn', 11, 0),
        ('turn', 2, 0),
        ('leaf', 1),
        ('first', 1),
        ('turn', 3, 2),
        ('turn', 0, 1),
        ('turn', 9, 0),
        ('turn', 1, 2),
        ('turn', 10, 0),
        ('turn', 2, 1),
        ('turn', 4, 0),
        ('turn', 11, 1),
        ('turn', 6, 1),
        ('turn', 8, 0),
        ('first', 13),
        ('turn', 3, 3),
        ('turn', 7, 2),
        ('first', 8),
        ('first', 15),
        ('turn', 5, 0),
        ('turn', 8, 1),
        ('turn', 0, 2),
        ('turn', 5, 1),
        ('turn', 2, 2),
        ('turn', 3, 4),
        ('turn', 11, 2),
        ('turn', 7, 3),
        ('turn', 1, 3),
        ('turn', 10, 1),
        ('turn', 0, 3),
        ('turn', 2, 3),
        ('turn', 9, 1),
        ('first', 6),
        ('turn', 8, 2),
        ('turn', 11, 3),
        ('turn', 6, 2),
        ('split', 0),
        ('turn', 7, 4),
        ('turn', 5, 2),
        ('split', 3),
        ('turn', 2, 4),
        ('first', 7),
        ('turn', 3, 5),
        ('first', 11),
        ('turn', 0, 4),
        ('turn', 10, 2),
        ('turn', 4, 1),
        ('turn', 8, 3),
        ('turn', 1, 4),
        ('turn', 5, 3),
        ('first', 10),
        ('turn', 11, 4),
        ('turn', 2, 5),
        ('turn', 3, 6),
        ('turn', 4, 2),
        ('turn', 0, 5),
        ('turn', 1, 5),
        ('split', 1),
        ('turn', 8, 4),
        ('turn', 3, 7),
        ('turn', 7, 5),
        ('turn', 9, 2),
        ('turn', 2, 6),
        ('turn', 6, 3),
        ('turn', 5, 4),
        ('turn', 4, 3),
        ('turn', 10, 3),
        ('split', 2),
        ('turn', 1, 6),
        ('turn', 11, 5),
        ('turn', 7, 6),
        ('turn', 0, 6),
        ('turn', 8, 5),
        ('turn', 3, 8),
        ('turn', 2, 7),
        ('contract', 0),
        ('turn', 6, 4),
        ('turn', 9, 3),
        ('turn', 5, 5),
        ('turn', 4, 4),
        ('turn', 11, 6),
        ('turn', 10, 4),
        ('turn', 1, 7),
        ('turn', 0, 7),
        ('second', 12),
        ('turn', 6, 5),
        ('contract', 2),
        ('turn', 8, 6),
        ('turn', 4, 5),
        ('turn', 5, 6),
        ('second', 10),
        ('turn', 11, 7),
        ('turn', 9, 4),
        ('second', 14),
        ('turn', 0, 8),
        ('turn', 8, 7),
        ('turn', 10, 5),
        ('turn', 4, 6),
        ('turn', 1, 8),
        ('turn', 2, 8),
        ('second', 8),
        ('contract', 1),
        ('turn', 6, 6),
        ('second', 5),
        ('second', 9),
        ('turn', 10, 6),
        ('turn', 9, 5),
        ('turn', 4, 7),
        ('second', 6),
        ('turn', 8, 8),
        ('turn', 5, 7),
        ('second', 13),
        ('turn', 9, 6),
        ('contract', 3),
        ('second', 15),
        ('turn', 10, 7),
        ('turn', 6, 7),
        ('second', 4),
        ('second', 2),
        ('turn', 7, 7),
        ('turn', 11, 8),
        ('turn', 5, 8),
        ('second', 11),
        ('second', 3),
        ('turn', 6, 8),
        ('turn', 10, 8),
        ('turn', 9, 7),
        ('turn', 4, 8),
        ('multiply',),
        ('second', 7),
        ('turn', 7, 8),
        ('second', 1),
        ('absorb', 1),
        ('absorb', 0),
        ('absorb', 2),
        ('turn', 9, 8),
        ('interleave',),
        ('absorb', 3),
    ]
    if n == 16:
        return TABLE
    return [event for _, event in sorted(events, key=lambda entry: entry[0])]


def network_kernel(
    n, bits, stem, left, right, mixed_out, absorbed_out,
    l0, l1, l2, l3, r0, r1, r2, r3, part, outgoing, incoming, branch, got0, planes, blocks1, got1, absorbed,
    q_product, mixed, wide, leaf_sem, own_sem, a_send, a_recv, r_send, r_recv,
):
    planes_in, _, span, columns = part.shape
    parts = pieces_of(planes_in, span)
    chunks = len(parts)
    width = n * span
    steps = n.bit_length() - 1
    group = n // 4
    me = lax.axis_index("outer")
    lefts, rights = (l0, l1, l2, l3), (r0, r1, r2, r3)

    bit = [lax.rem(me // (1 << s), 2) for s in range(steps)]

    def flipped(k):
        return sum((1 - bit[s] if k >> s & 1 else bit[s]) * (1 << s) for s in range(steps))

    def reversed_bits(k):
        return sum(lax.rem(k // (1 << s), 2) * (n >> (s + 1)) for s in range(steps))

    partners = [me + (1 << s) * (1 - 2 * bit[s]) for s in range(steps)]
    starts = [0]
    gives = []
    for s in range(steps):
        half = n >> (s + 1)
        gives.append(starts[s] + (1 - bit[s]) * half)
        starts.append(starts[s] + bit[s] * half)

    barrier = pltpu.get_barrier_semaphore()

    def greet(k, carry):
        pl.semaphore_signal(barrier, inc=1, device_id={"outer": lax.rem(me + k, n)}, device_id_type=MESH)
        return carry

    lax.fori_loop(1, n, greet, 0)

    def leaf_copies(j):
        return (
            pltpu.make_async_copy(left.at[j], lefts[j], leaf_sem.at[j, 0]),
            pltpu.make_async_copy(right.at[j], rights[j], leaf_sem.at[j, 1]),
        )

    def first_copy(k):
        to = flipped(k)
        return pltpu.make_async_remote_copy(
            src_ref=stem.at[to], dst_ref=got0.at[me], send_sem=a_send.at[k], recv_sem=a_recv.at[0, k // group],
            device_id={"outer": to}, device_id_type=MESH)

    def second_copy(k):
        to = flipped(k)
        return pltpu.make_async_remote_copy(
            src_ref=blocks1.at[reversed_bits(to)], dst_ref=got1.at[me // 4, lax.rem(me, 4)],
            send_sem=a_send.at[k], recv_sem=a_recv.at[1, k % 4],
            device_id={"outer": to}, device_id_type=MESH)

    own_copy = pltpu.make_async_copy(stem.at[me], got0.at[me], a_recv.at[0, 0])

    unsettled = {}

    def launch(copy, *slot):
        if slot in unsettled:
            unsettled[slot].wait_send()
        copy.start()
        unsettled[slot] = copy

    def send_first(k):
        launch(first_copy(k), k)

    def send_second(k):
        launch(second_copy(k), k)

    def split(i):
        here = pl.ds(flipped(group * i) // group * group, group)
        pltpu.make_async_copy(got0.at[here], got0.at[here], a_recv.at[0, i]).wait()
        rows = group * span
        entries = got0[here].reshape(2 * rows, columns).astype(jnp.float32)
        for t in range(columns // LANES):
            lanes = slice(t * LANES, (t + 1) * LANES)
            wide[t, 0 : 2 * rows] = entries[:, lanes]
            for p in range(2):
                plane = wide[t, pl.ds(p, rows, stride=2), :]
                planes[p, here, :, lanes] = plane.astype(jnp.bfloat16).reshape(group, span, LANES)

    def dot(a, b):
        return jnp.dot(a, b, preferred_element_type=jnp.float32)

    def leaf_product(j):
        for copy in leaf_copies(j):
            copy.wait()
        chosen = bits[j]
        plain_ref, other_ref = (rights[j], lefts[j]) if j % 2 == 0 else (lefts[j], rights[j])
        rows = 2 * plain_ref.shape[1]
        plain = plain_ref[chosen].reshape(rows, plain_ref.shape[3])
        other = other_ref[chosen].reshape(rows, other_ref.shape[3]).astype(jnp.float32)
        even = lax.rem(lax.broadcasted_iota(jnp.int32, other.shape, 0), 2) == 0
        signed = jnp.where(even, other, -other).astype(jnp.bfloat16)
        swapped = jnp.where(even, pltpu.roll(other, rows - 1, 0), pltpu.roll(other, 1, 0)).astype(jnp.bfloat16)
        dims = (((0,), (0,)), ((), ()))
        for p, factor in enumerate((signed, swapped)):
            product = lax.dot_general(plain, factor, dims, preferred_element_type=jnp.float32)
            product = product.reshape(n, span, columns)
            if j == 0:
                for b in range(n):
                    at = sum((b >> s & 1) * (n >> (s + 1)) for s in range(steps))
                    part[p, at] = product[b]
            else:
                part[2 * j + p] = product

    def reduce_copy(c, s):
        half, at = n >> (s + 1), n - (n >> s)
        plane, rows = parts[c]
        return pltpu.make_async_remote_copy(
            src_ref=outgoing.at[plane, pl.ds(gives[s], half), rows], dst_ref=incoming.at[plane, pl.ds(at, half), rows],
            send_sem=r_send.at[c], recv_sem=r_recv.at[c, s],
            device_id={"outer": partners[s]}, device_id_type=MESH)

    def gather_copy(c, s, first):
        plane, rows = parts[c]
        here = branch.at[plane, pl.ds(first, n >> (s + 1)), rows]
        return pltpu.make_async_remote_copy(
            src_ref=here, dst_ref=here, send_sem=r_send.at[c], recv_sem=r_recv.at[c, 2 * steps - 1 - s],
            device_id={"outer": partners[s]}, device_id_type=MESH)

    def begin(c, step):
        if step < steps:
            plane, rows = parts[c]
            give = pl.ds(gives[step], n >> (step + 1))
            outgoing[plane, give, rows] = part[plane, give, rows].astype(outgoing.dtype)
            launch(reduce_copy(c, step), 'chunk', c)
        else:
            s = 2 * steps - 1 - step
            launch(gather_copy(c, s, starts[s + 1]), 'chunk', c)

    def finish(c, step):
        if step < steps:
            plane, rows = parts[c]
            half, at = n >> (step + 1), n - (n >> step)
            reduce_copy(c, step).wait_recv()
            keep = pl.ds(starts[step + 1], half)
            total = part[plane, keep, rows] + incoming[plane, pl.ds(at, half), rows].astype(jnp.float32)
            if step == steps - 1:
                branch[plane, keep, rows] = total.astype(branch.dtype)
            else:
                part[plane, keep, rows] = total
        else:
            s = 2 * steps - 1 - step
            gather_copy(c, s, gives[s]).wait_recv()

    def turn(c, step):
        if step:
            finish(c, step - 1)
        if step < 2 * steps:
            begin(c, step)

    def near(low):
        core = lax.rem(bit[0] + low % 2, 2)
        side = lax.rem(bit[1] + low // 2, 2)
        return core, side

    def contract_first(low):
        core, side = near(low)
        here = pl.ds(core * (n // 2) + side * (n // 4), group)
        p_real = branch[0, here].reshape(group * span, width)
        p_imag = branch[1, here].reshape(group * span, width)
        a_real, a_imag = planes[0].reshape(width, columns), planes[1].reshape(width, columns)
        real_part = (dot(p_real, a_real) - dot(p_imag, a_imag)).astype(jnp.bfloat16)
        imag_part = (dot(p_real, a_imag) + dot(p_imag, a_real)).astype(jnp.bfloat16)
        blocks1[here, 0:span] = real_part.reshape(group, span, columns)
        blocks1[here, span : 2 * span] = imag_part.reshape(group, span, columns)
        if low == 0:
            got1[me // 4, lax.rem(me, 4)] = blocks1[starts[steps]]

    stored = []

    def put(source, target, semaphore):
        copy = pltpu.make_async_copy(source, target, semaphore)
        copy.start()
        stored.append(copy)

    def interleave():
        for t in range(width // LANES):
            lanes = slice(t * LANES, (t + 1) * LANES)
            p_real, p_imag = (
                branch[4 + p, :, :, lanes].reshape(width, LANES).astype(jnp.float32) for p in range(2))
            for k, (even, odd) in enumerate(((p_real, p_imag), (-p_imag, p_real))):
                wide[t, pl.ds(0, width, stride=2), :] = even
                wide[t, pl.ds(1, width, stride=2), :] = odd
                mixed[k, :, lanes] = wide[t].astype(jnp.bfloat16)
        put(mixed, mixed_out, own_sem)

    def multiply():
        a_real, a_imag, b_real, b_imag = (branch[c].reshape(width, columns) for c in (2, 3, 6, 7))
        q_product[0] = (dot(a_real, b_real) - dot(a_imag, b_imag)).astype(jnp.bfloat16)
        q_product[1] = (dot(a_real, b_imag) + dot(a_imag, b_real)).astype(jnp.bfloat16)

    def absorb(low):
        fill = got1.at[pl.ds(0, group if low else group - 1), 0]
        pltpu.make_async_copy(fill, fill, a_recv.at[1, low]).wait()
        core, side = near(low)
        entries = got1[:, core + 2 * side].reshape(group * 2 * span, columns)
        by_real = dot(entries, q_product[0]).reshape(group, 2, span, columns)
        by_imag = dot(entries, q_product[1]).reshape(group, 2, span, columns)
        absorbed[0, :, core + 2 * side] = (by_real[:, 0] - by_imag[:, 1]).astype(absorbed.dtype)
        absorbed[1, :, core + 2 * side] = (by_imag[:, 0] + by_real[:, 1]).astype(absorbed.dtype)
        for p in range(2):
            put(absorbed.at[p, :, core + 2 * side], absorbed_out.at[p, :, core + 2 * side], leaf_sem.at[low, p])

    for copy in leaf_copies(0):
        copy.start()
    own_copy.start()
    leaf_product(0)
    for j in LEAF_ORDER:
        for copy in leaf_copies(j):
            copy.start()
    pl.semaphore_wait(barrier, n - 1)

    acts = dict(
        leaf=leaf_product, turn=turn, first=send_first, split=split, contract=contract_first, second=send_second,
        interleave=interleave, multiply=multiply, absorb=absorb)
    for name, *arguments in schedule(n, steps, parts):
        acts[name](*arguments)

    for copy in unsettled.values():
        copy.wait_send()
    for copy in stored:
        copy.wait()


def last_kernel(mixed, absorbed, out, mixed_here, absorbed_here, out_here, semaphores):
    rows = mixed.shape[1] // TILES
    copies = []
    for tile in range(TILES):
        here = pl.ds(tile * rows, rows)
        copies.append(pltpu.make_async_copy(mixed.at[:, here], mixed_here.at[:, here], semaphores.at[tile]))
    fetch = pltpu.make_async_copy(absorbed, absorbed_here, semaphores.at[TILES])
    copies[0].start()
    fetch.start()
    for copy in copies[1:]:
        copy.start()
    stores = []
    for tile, copy in enumerate(copies):
        copy.wait()
        if tile == 0:
            fetch.wait()
        here = pl.ds(tile * rows, rows)
        half = pl.ds(tile * (rows // 2), rows // 2)
        total = jnp.dot(mixed_here[0, here], absorbed_here[0], preferred_element_type=jnp.float32)
        total = total + jnp.dot(mixed_here[1, here], absorbed_here[1], preferred_element_type=jnp.float32)
        out_here[half] = total.astype(out.dtype).reshape(rows // 2, 2, out.shape[2])
        stores.append(pltpu.make_async_copy(out_here.at[half], out.at[half], semaphores.at[tile]))
        stores[-1].start()
    for store in stores:
        store.wait()


def contract_last(mixed, absorbed):
    _, rows, width = mixed.shape
    columns = absorbed.shape[2]
    anywhere = pl.BlockSpec(memory_space=pl.ANY)
    return pl.pallas_call(
        last_kernel,
        out_shape=jax.ShapeDtypeStruct((rows // 2, 2, columns), jnp.bfloat16),
        in_specs=[anywhere, anywhere],
        out_specs=anywhere,
        scratch_shapes=[
            pltpu.VMEM(mixed.shape, mixed.dtype),
            pltpu.VMEM(absorbed.shape, absorbed.dtype),
            pltpu.VMEM((rows // 2, 2, columns), jnp.bfloat16),
            pltpu.SemaphoreType.DMA((TILES + 1,)),
        ],
    )(mixed, absorbed)


def on_device(n, stem_tensor, leaf_left, leaf_right, slice_bits):
    branches, slices, depth, _, rows = leaf_left.shape
    width, columns = stem_tensor.shape[1], stem_tensor.shape[3]
    span = width // n
    steps = n.bit_length() - 1
    chunks = len(pieces_of(2 * branches, span))
    blocks = stem_tensor.reshape(n, span, 2, columns)
    both = (2 * branches, n, span, columns)
    anywhere = pl.BlockSpec(memory_space=pl.ANY)
    mixed, absorbed = pl.pallas_call(
        functools.partial(network_kernel, n),
        out_shape=(
            jax.ShapeDtypeStruct((2, 2 * width, width), jnp.bfloat16),
            jax.ShapeDtypeStruct((2, n // 4, 4, span, columns), jnp.bfloat16),
        ),
        in_specs=[pl.BlockSpec(memory_space=pltpu.SMEM), anywhere, anywhere, anywhere],
        out_specs=(anywhere, anywhere),
        scratch_shapes=[
            *[pltpu.VMEM((slices, depth, 2, rows), jnp.bfloat16)] * branches,
            *[pltpu.VMEM((slices, depth, 2, columns), jnp.bfloat16)] * branches,
            pltpu.VMEM(both, jnp.float32),
            pltpu.VMEM(both, jnp.bfloat16),
            pltpu.VMEM(both, jnp.bfloat16),
            pltpu.VMEM(both, jnp.bfloat16),
            pltpu.VMEM((n, span, 2, columns), jnp.bfloat16),
            pltpu.VMEM((2, n, span, columns), jnp.bfloat16),
            pltpu.VMEM((n, 2 * span, columns), jnp.bfloat16),
            pltpu.VMEM((n // 4, 4, 2 * span, columns), jnp.bfloat16),
            pltpu.VMEM((2, n // 4, 4, span, columns), jnp.bfloat16),
            pltpu.VMEM((2, width, columns), jnp.bfloat16),
            pltpu.VMEM((2, 2 * width, columns), jnp.bfloat16),
            pltpu.VMEM((columns // LANES, 2 * width, LANES), jnp.float32),
            pltpu.SemaphoreType.DMA((branches, 2)),
            pltpu.SemaphoreType.DMA,
            pltpu.SemaphoreType.DMA((n,)),
            pltpu.SemaphoreType.DMA((2, 4)),
            pltpu.SemaphoreType.DMA((chunks,)),
            pltpu.SemaphoreType.DMA((chunks, 2 * steps)),
        ],
        compiler_params=pltpu.CompilerParams(
            collective_id=0, has_side_effects=True, vmem_limit_bytes=60 * 1024 * 1024),
    )(slice_bits, blocks, leaf_left, leaf_right)
    return contract_last(mixed, absorbed.reshape(2, width, columns))[None]


def solution(mesh):
    return jax.shard_map(
        functools.partial(on_device, mesh.shape["outer"]),
        mesh=mesh,
        in_specs=(
            P(("cuts", "outer"), None, None, None),
            P(None, None, "outer", None, None),
            P(None, None, "outer", None, None),
            P("cuts"),
        ),
        out_specs=P(("cuts", "outer"), None, None, None),
        check_vma=False,
    )
```

```python
import functools

import jax
import jax.numpy as jnp
from jax import lax
from jax.experimental import pallas as pl
from jax.experimental.pallas import tpu as pltpu
from jax.sharding import PartitionSpec as P

MESH = pl.DeviceIdType.MESH
LANES = 128
TILES = 4
HALVES = 1
LEAF_ORDER = (3, 2, 1)
PIECES = (2, 1, 2, 1)


STAGES = (1.6, 4.5, 3.5, 3.5)
ENTRIES = (0.5, 15.0, 7.0, 20.0)
GAP = 0.4
TABLE = [
    ('first', 14),
    ('turn', 0, 0),
    ('turn', 3, 0),
    ('leaf', 3),
    ('turn', 2, 0),
    ('first', 15),
    ('turn', 0, 1),
    ('turn', 1, 0),
    ('first', 5),
    ('first', 12),
    ('first', 4),
    ('turn', 2, 1),
    ('leaf', 2),
    ('turn', 3, 1),
    ('first', 1),
    ('turn', 8, 0),
    ('leaf', 1),
    ('turn', 1, 1),
    ('turn', 6, 0),
    ('turn', 0, 2),
    ('turn', 8, 1),
    ('first', 8),
    ('turn', 4, 0),
    ('turn', 7, 0),
    ('turn', 2, 2),
    ('first', 10),
    ('turn', 7, 1),
    ('turn', 0, 3),
    ('turn', 5, 0),
    ('turn', 3, 2),
    ('first', 9),
    ('turn', 1, 2),
    ('turn', 11, 0),
    ('turn', 6, 1),
    ('turn', 2, 3),
    ('turn', 4, 1),
    ('turn', 7, 2),
    ('turn', 3, 3),
    ('turn', 10, 0),
    ('turn', 5, 1),
    ('turn', 8, 2),
    ('turn', 0, 4),
    ('turn', 6, 2),
    ('turn', 7, 3),
    ('turn', 1, 3),
    ('first', 7),
    ('turn', 9, 0),
    ('turn', 4, 2),
    ('turn', 8, 3),
    ('turn', 0, 5),
    ('turn', 11, 1),
    ('turn', 2, 4),
    ('turn', 1, 4),
    ('turn', 5, 2),
    ('turn', 8, 4),
    ('turn', 3, 4),
    ('turn', 6, 3),
    ('turn', 11, 2),
    ('turn', 9, 1),
    ('first', 2),
    ('first', 6),
    ('turn', 4, 3),
    ('turn', 5, 3),
    ('turn', 3, 5),
    ('turn', 10, 1),
    ('turn', 6, 4),
    ('turn', 2, 5),
    ('first', 13),
    ('turn', 1, 5),
    ('turn', 11, 3),
    ('turn', 9, 2),
    ('split', 1),
    ('first', 3),
    ('turn', 3, 6),
    ('turn', 6, 5),
    ('turn', 4, 4),
    ('turn', 8, 5),
    ('turn', 2, 6),
    ('turn', 10, 2),
    ('turn', 5, 4),
    ('first', 11),
    ('turn', 0, 6),
    ('turn', 4, 5),
    ('turn', 3, 7),
    ('turn', 1, 6),
    ('turn', 9, 3),
    ('turn', 2, 7),
    ('turn', 7, 4),
    ('turn', 8, 6),
    ('turn', 0, 7),
    ('turn', 3, 8),
    ('turn', 10, 3),
    ('turn', 5, 5),
    ('turn', 6, 6),
    ('turn', 9, 4),
    ('turn', 11, 4),
    ('split', 0),
    ('turn', 4, 6),
    ('turn', 0, 8),
    ('turn', 1, 7),
    ('split', 2),
    ('turn', 2, 8),
    ('turn', 7, 5),
    ('split', 3),
    ('contract', 2),
    ('turn', 10, 4),
    ('turn', 1, 8),
    ('turn', 5, 6),
    ('second', 14),
    ('turn', 11, 5),
    ('second', 10),
    ('contract', 0),
    ('contract', 3),
    ('turn', 10, 5),
    ('second', 12),
    ('second', 8),
    ('turn', 7, 6),
    ('contract', 1),
    ('turn', 11, 6),
    ('turn', 9, 5),
    ('turn', 10, 6),
    ('turn', 6, 7),
    ('turn', 7, 7),
    ('turn', 8, 7),
    ('second', 6),
    ('turn', 9, 6),
    ('second', 13),
    ('second', 5),
    ('turn', 4, 7),
    ('second', 11),
    ('turn', 5, 7),
    ('second', 15),
    ('turn', 4, 8),
    ('turn', 8, 8),
    ('turn', 7, 8),
    ('second', 4),
    ('turn', 11, 7),
    ('turn', 10, 7),
    ('second', 7),
    ('second', 1),
    ('turn', 11, 8),
    ('second', 2),
    ('second', 9),
    ('turn', 9, 7),
    ('turn', 10, 8),
    ('second', 3),
    ('turn', 6, 8),
    ('turn', 5, 8),
    ('multiply',),
    ('turn', 9, 8),
    ('absorb', 0),
    ('interleave',),
    ('absorb', 2),
    ('absorb', 3),
    ('absorb', 1),
]


def pieces_of(planes, span):
    parts = []
    for plane in range(planes):
        pieces = PIECES[plane // 2] if span % 32 == 0 else 1
        parts += [(plane, pl.ds(h * (span // pieces), span // pieces)) for h in range(pieces)]
    return parts


def schedule(n, steps, parts):
    if n == 16:
        return TABLE
    events = []

    def at(time, *event):
        events.append((time, event))

    stages = [STAGES[min(s, 3)] for s in range(steps)]
    stages = stages + stages[::-1]
    done = {}
    for c, (plane, _) in enumerate(parts):
        begin = ENTRIES[plane // 2] + GAP * (plane % 2)
        for step in range(2 * steps + 1):
            done[c, step] = begin + sum(stages[:step])
            at(done[c, step], "turn", c, step)
    chunks_of = [[c for c, (plane, _) in enumerate(parts) if plane // 2 == j] for j in range(4)]
    for j in LEAF_ORDER:
        at(ENTRIES[j] - 1, "leaf", j)
    ready = max(done[c, 2 * steps - 2] for c in chunks_of[0])
    for k in range(1, n):
        at(ready * k / (2 * n), "first", k)
    for i in range(4):
        at(ready * (i + 5) / 10, "split", i)
    for low, s in ((0, 2), (2, 1), (1, 0), (3, 0)):
        time = max(done[c, 2 * steps - s] for c in chunks_of[0]) + 0.01 * (1 + low)
        at(time, "contract", low)
        for q in range(n // 4):
            if q or low:
                at(time, "second", 4 * q + low)
    end = max(done.values()) + 1
    at(end, "interleave")
    at(end, "multiply")
    for i, low in enumerate((0, 2, 1, 3)):
        at(end + i + 1, "absorb", low)
    return [event for _, event in sorted(events, key=lambda entry: entry[0])]


def network_kernel(
    n, bits_in, stem, left, right, mixed_out, absorbed_out,
    bits,    l0, l1, l2, l3, r0, r1, r2, r3, part, outgoing, incoming, branch, got0, planes, blocks1, got1, absorbed,
    q_product, mixed, wide, leaf_sem, own_sem, a_send, a_recv, r_send, r_recv,
):
    planes_in, _, span, columns = part.shape
    parts = pieces_of(planes_in, span)
    chunks = len(parts)
    width = n * span
    steps = n.bit_length() - 1
    group = n // 4
    me = lax.axis_index("outer")
    lefts, rights = (l0, l1, l2, l3), (r0, r1, r2, r3)

    bit = [lax.rem(me // (1 << s), 2) for s in range(steps)]

    def flipped(k):
        return sum((1 - bit[s] if k >> s & 1 else bit[s]) * (1 << s) for s in range(steps))

    def reversed_bits(k):
        return sum(lax.rem(k // (1 << s), 2) * (n >> (s + 1)) for s in range(steps))

    partners = [me + (1 << s) * (1 - 2 * bit[s]) for s in range(steps)]
    starts = [0]
    gives = []
    for s in range(steps):
        half = n >> (s + 1)
        gives.append(starts[s] + (1 - bit[s]) * half)
        starts.append(starts[s] + bit[s] * half)

    barrier = pltpu.get_barrier_semaphore()

    def greet(k, carry):
        pl.semaphore_signal(barrier, inc=1, device_id={"outer": lax.rem(me + k, n)}, device_id_type=MESH)
        return carry

    lax.fori_loop(1, n, greet, 0)
    bits_copy = pltpu.make_async_copy(bits_in, bits, own_sem)
    bits_copy.start()

    depth = l0.shape[1]

    def leaf_copies(j, piece=0, pieces=1):
        here = pl.ds(piece * (depth // pieces), depth // pieces)
        return (
            pltpu.make_async_copy(left.at[j, :, here], lefts[j].at[:, here], leaf_sem.at[j + piece, 0]),
            pltpu.make_async_copy(right.at[j, :, here], rights[j].at[:, here], leaf_sem.at[j + piece, 1]),
        )

    def first_copy(k):
        to = flipped(k)
        return pltpu.make_async_remote_copy(
            src_ref=stem.at[to], dst_ref=got0.at[me], send_sem=a_send.at[k], recv_sem=a_recv.at[0, k // group],
            device_id={"outer": to}, device_id_type=MESH)

    def second_copy(k):
        to = flipped(k)
        return pltpu.make_async_remote_copy(
            src_ref=blocks1.at[reversed_bits(to)], dst_ref=got1.at[me // 4, lax.rem(me, 4)],
            send_sem=a_send.at[k], recv_sem=a_recv.at[1, k % 4],
            device_id={"outer": to}, device_id_type=MESH)

    own_copy = pltpu.make_async_copy(stem.at[me], got0.at[me], a_recv.at[0, 0])

    unsettled = {}

    def launch(copy, *slot):
        if slot in unsettled:
            unsettled[slot].wait_send()
        copy.start()
        unsettled[slot] = copy

    def send_first(k):
        launch(first_copy(k), k)

    def send_second(k):
        launch(second_copy(k), k)

    def split(i):
        here = pl.ds(flipped(group * i) // group * group, group)
        pltpu.make_async_copy(got0.at[here], got0.at[here], a_recv.at[0, i]).wait()
        rows = group * span
        entries = got0[here].reshape(2 * rows, columns).astype(jnp.float32)
        for t in range(columns // LANES):
            lanes = slice(t * LANES, (t + 1) * LANES)
            wide[t, 0 : 2 * rows] = entries[:, lanes]
            for p in range(2):
                plane = wide[t, pl.ds(p, rows, stride=2), :]
                planes[p, here, :, lanes] = plane.astype(jnp.bfloat16).reshape(group, span, LANES)

    def dot(a, b):
        return jnp.dot(a, b, preferred_element_type=jnp.float32)

    def leaf_product(j, piece=0, pieces=1):
        for copy in leaf_copies(j, piece, pieces):
            copy.wait()
        if j == 0 and piece == pieces - 1:
            for other in LEAF_ORDER:
                for copy in leaf_copies(other):
                    copy.start()
        chosen = bits[j]
        plain_ref, other_ref = (rights[j], lefts[j]) if j % 2 == 0 else (lefts[j], rights[j])
        here = pl.ds(piece * (depth // pieces), depth // pieces)
        rows = 2 * depth // pieces
        plain = plain_ref[chosen, here].reshape(rows, plain_ref.shape[3])
        other = other_ref[chosen, here].reshape(rows, other_ref.shape[3]).astype(jnp.float32)
        even = lax.rem(lax.broadcasted_iota(jnp.int32, other.shape, 0), 2) == 0
        signed = jnp.where(even, other, -other).astype(jnp.bfloat16)
        swapped = jnp.where(even, pltpu.roll(other, rows - 1, 0), pltpu.roll(other, 1, 0)).astype(jnp.bfloat16)
        dims = (((0,), (0,)), ((), ()))
        for p, factor in enumerate((signed, swapped)):
            product = lax.dot_general(plain, factor, dims, preferred_element_type=jnp.float32)
            product = product.reshape(n, span, columns)
            for b in range(n if j == 0 else 0):
                at = sum((b >> s & 1) * (n >> (s + 1)) for s in range(steps))
                if piece:
                    part[p, at] += product[b]
                else:
                    part[p, at] = product[b]
            if j:
                part[2 * j + p] = product

    def reduce_copy(c, s):
        half, at = n >> (s + 1), n - (n >> s)
        plane, rows = parts[c]
        return pltpu.make_async_remote_copy(
            src_ref=outgoing.at[plane, pl.ds(gives[s], half), rows], dst_ref=incoming.at[plane, pl.ds(at, half), rows],
            send_sem=r_send.at[c], recv_sem=r_recv.at[c, s],
            device_id={"outer": partners[s]}, device_id_type=MESH)

    def gather_copy(c, s, first):
        plane, rows = parts[c]
        here = branch.at[plane, pl.ds(first, n >> (s + 1)), rows]
        return pltpu.make_async_remote_copy(
            src_ref=here, dst_ref=here, send_sem=r_send.at[c], recv_sem=r_recv.at[c, 2 * steps - 1 - s],
            device_id={"outer": partners[s]}, device_id_type=MESH)

    def begin(c, step):
        if step < steps:
            plane, rows = parts[c]
            give = pl.ds(gives[step], n >> (step + 1))
            outgoing[plane, give, rows] = part[plane, give, rows].astype(outgoing.dtype)
            launch(reduce_copy(c, step), 'chunk', c)
        else:
            s = 2 * steps - 1 - step
            launch(gather_copy(c, s, starts[s + 1]), 'chunk', c)

    def finish(c, step):
        if step < steps:
            plane, rows = parts[c]
            half, at = n >> (step + 1), n - (n >> step)
            reduce_copy(c, step).wait_recv()
            keep = pl.ds(starts[step + 1], half)
            total = part[plane, keep, rows] + incoming[plane, pl.ds(at, half), rows].astype(jnp.float32)
            if step == steps - 1:
                branch[plane, keep, rows] = total.astype(branch.dtype)
            else:
                part[plane, keep, rows] = total
        else:
            s = 2 * steps - 1 - step
            gather_copy(c, s, gives[s]).wait_recv()

    def turn(c, step):
        if step:
            finish(c, step - 1)
        if step < 2 * steps:
            begin(c, step)

    def near(low):
        core = lax.rem(bit[0] + low % 2, 2)
        side = lax.rem(bit[1] + low // 2, 2)
        return core, side

    def contract_first(low):
        core, side = near(low)
        here = pl.ds(core * (n // 2) + side * (n // 4), group)
        p_real = branch[0, here].reshape(group * span, width)
        p_imag = branch[1, here].reshape(group * span, width)
        a_real, a_imag = planes[0].reshape(width, columns), planes[1].reshape(width, columns)
        real_part = (dot(p_real, a_real) - dot(p_imag, a_imag)).astype(jnp.bfloat16)
        imag_part = (dot(p_real, a_imag) + dot(p_imag, a_real)).astype(jnp.bfloat16)
        blocks1[here, 0:span] = real_part.reshape(group, span, columns)
        blocks1[here, span : 2 * span] = imag_part.reshape(group, span, columns)
        if low == 0:
            got1[me // 4, lax.rem(me, 4)] = blocks1[starts[steps]]

    stored = []

    def put(source, target, semaphore):
        copy = pltpu.make_async_copy(source, target, semaphore)
        copy.start()
        stored.append(copy)

    def interleave():
        for t in range(width // LANES):
            lanes = slice(t * LANES, (t + 1) * LANES)
            p_real, p_imag = (
                branch[4 + p, :, :, lanes].reshape(width, LANES).astype(jnp.float32) for p in range(2))
            for k, (even, odd) in enumerate(((p_real, p_imag), (-p_imag, p_real))):
                wide[t, pl.ds(0, width, stride=2), :] = even
                wide[t, pl.ds(1, width, stride=2), :] = odd
                mixed[k, :, lanes] = wide[t].astype(jnp.bfloat16)
        put(mixed, mixed_out, own_sem)

    def multiply():
        a_real, a_imag, b_real, b_imag = (branch[c].reshape(width, columns) for c in (2, 3, 6, 7))
        q_product[0] = (dot(a_real, b_real) - dot(a_imag, b_imag)).astype(jnp.bfloat16)
        q_product[1] = (dot(a_real, b_imag) + dot(a_imag, b_real)).astype(jnp.bfloat16)

    def absorb(low):
        fill = got1.at[pl.ds(0, group if low else group - 1), 0]
        pltpu.make_async_copy(fill, fill, a_recv.at[1, low]).wait()
        core, side = near(low)
        entries = got1[:, core + 2 * side].reshape(group * 2 * span, columns)
        by_real = dot(entries, q_product[0]).reshape(group, 2, span, columns)
        by_imag = dot(entries, q_product[1]).reshape(group, 2, span, columns)
        absorbed[0, :, core + 2 * side] = (by_real[:, 0] - by_imag[:, 1]).astype(absorbed.dtype)
        absorbed[1, :, core + 2 * side] = (by_imag[:, 0] + by_real[:, 1]).astype(absorbed.dtype)
        for p in range(2):
            put(absorbed.at[p, :, core + 2 * side], absorbed_out.at[p, :, core + 2 * side], leaf_sem.at[low, p])

    for piece in range(HALVES):
        for copy in leaf_copies(0, piece, HALVES):
            copy.start()
    own_copy.start()
    bits_copy.wait()
    for piece in range(HALVES):
        leaf_product(0, piece, HALVES)
    pl.semaphore_wait(barrier, n - 1)

    acts = dict(
        leaf=leaf_product, turn=turn, first=send_first, split=split, contract=contract_first, second=send_second,
        interleave=interleave, multiply=multiply, absorb=absorb)
    for name, *arguments in schedule(n, steps, parts):
        acts[name](*arguments)

    for copy in unsettled.values():
        copy.wait_send()
    for copy in stored:
        copy.wait()


def last_kernel(mixed, absorbed, out, mixed_here, absorbed_here, out_here, semaphores):
    rows = mixed.shape[1] // TILES
    copies = []
    for tile in range(TILES):
        here = pl.ds(tile * rows, rows)
        copies.append(pltpu.make_async_copy(mixed.at[:, here], mixed_here.at[:, here], semaphores.at[tile]))
    fetch = pltpu.make_async_copy(absorbed, absorbed_here, semaphores.at[TILES])
    copies[0].start()
    fetch.start()
    for copy in copies[1:]:
        copy.start()
    stores = []
    for tile, copy in enumerate(copies):
        copy.wait()
        if tile == 0:
            fetch.wait()
        here = pl.ds(tile * rows, rows)
        half = pl.ds(tile * (rows // 2), rows // 2)
        total = jnp.dot(mixed_here[0, here], absorbed_here[0], preferred_element_type=jnp.float32)
        total = total + jnp.dot(mixed_here[1, here], absorbed_here[1], preferred_element_type=jnp.float32)
        out_here[half] = total.astype(out.dtype).reshape(rows // 2, 2, out.shape[2])
        stores.append(pltpu.make_async_copy(out_here.at[half], out.at[half], semaphores.at[tile]))
        stores[-1].start()
    for store in stores:
        store.wait()


def contract_last(mixed, absorbed):
    _, rows, width = mixed.shape
    columns = absorbed.shape[2]
    anywhere = pl.BlockSpec(memory_space=pl.ANY)
    return pl.pallas_call(
        last_kernel,
        out_shape=jax.ShapeDtypeStruct((rows // 2, 2, columns), jnp.bfloat16),
        in_specs=[anywhere, anywhere],
        out_specs=anywhere,
        scratch_shapes=[
            pltpu.VMEM(mixed.shape, mixed.dtype),
            pltpu.VMEM(absorbed.shape, absorbed.dtype),
            pltpu.VMEM((rows // 2, 2, columns), jnp.bfloat16),
            pltpu.SemaphoreType.DMA((TILES + 1,)),
        ],
    )(mixed, absorbed)


def on_device(n, stem_tensor, leaf_left, leaf_right, slice_bits):
    branches, slices, depth, _, rows = leaf_left.shape
    width, columns = stem_tensor.shape[1], stem_tensor.shape[3]
    span = width // n
    steps = n.bit_length() - 1
    chunks = len(pieces_of(2 * branches, span))
    blocks = stem_tensor.reshape(n, span, 2, columns)
    both = (2 * branches, n, span, columns)
    anywhere = pl.BlockSpec(memory_space=pl.ANY)
    mixed, absorbed = pl.pallas_call(
        functools.partial(network_kernel, n),
        out_shape=(
            jax.ShapeDtypeStruct((2, 2 * width, width), jnp.bfloat16),
            jax.ShapeDtypeStruct((2, n // 4, 4, span, columns), jnp.bfloat16),
        ),
        in_specs=[anywhere, anywhere, anywhere, anywhere],
        out_specs=(anywhere, anywhere),
        scratch_shapes=[
            pltpu.SMEM((branches,), jnp.int32),
            *[pltpu.VMEM((slices, depth, 2, rows), jnp.bfloat16)] * branches,
            *[pltpu.VMEM((slices, depth, 2, columns), jnp.bfloat16)] * branches,
            pltpu.VMEM(both, jnp.float32),
            pltpu.VMEM(both, jnp.bfloat16),
            pltpu.VMEM(both, jnp.bfloat16),
            pltpu.VMEM(both, jnp.bfloat16),
            pltpu.VMEM((n, span, 2, columns), jnp.bfloat16),
            pltpu.VMEM((2, n, span, columns), jnp.bfloat16),
            pltpu.VMEM((n, 2 * span, columns), jnp.bfloat16),
            pltpu.VMEM((n // 4, 4, 2 * span, columns), jnp.bfloat16),
            pltpu.VMEM((2, n // 4, 4, span, columns), jnp.bfloat16),
            pltpu.VMEM((2, width, columns), jnp.bfloat16),
            pltpu.VMEM((2, 2 * width, columns), jnp.bfloat16),
            pltpu.VMEM((columns // LANES, 2 * width, LANES), jnp.float32),
            pltpu.SemaphoreType.DMA((branches, 2)),
            pltpu.SemaphoreType.DMA,
            pltpu.SemaphoreType.DMA((n,)),
            pltpu.SemaphoreType.DMA((2, 4)),
            pltpu.SemaphoreType.DMA((chunks,)),
            pltpu.SemaphoreType.DMA((chunks, 2 * steps)),
        ],
        compiler_params=pltpu.CompilerParams(
            collective_id=0, has_side_effects=True, vmem_limit_bytes=60 * 1024 * 1024),
    )(slice_bits, blocks, leaf_left, leaf_right)
    return contract_last(mixed, absorbed.reshape(2, width, columns))[None]


def solution(mesh):
    return jax.shard_map(
        functools.partial(on_device, mesh.shape["outer"]),
        mesh=mesh,
        in_specs=(
            P(("cuts", "outer"), None, None, None),
            P(None, None, "outer", None, None),
            P(None, None, "outer", None, None),
            P("cuts"),
        ),
        out_specs=P(("cuts", "outer"), None, None, None),
        check_vma=False,
    )
```

```python
import functools

import jax
import jax.numpy as jnp
from jax import lax
from jax.experimental import pallas as pl
from jax.experimental.pallas import tpu as pltpu
from jax.sharding import PartitionSpec as P

MESH = pl.DeviceIdType.MESH
LANES = 128
TILES = 4
HALVES = 2
LEAF_ORDER = (3, 2, 1)
PIECES = (2, 1, 2, 1)


STAGES = (1.6, 4.5, 3.5, 3.5)
ENTRIES = (0.5, 15.0, 7.0, 20.0)
GAP = 0.4
TABLE = [
    ('first', 14),
    ('turn', 0, 0),
    ('turn', 3, 0),
    ('leaf', 3),
    ('turn', 2, 0),
    ('first', 15),
    ('turn', 0, 1),
    ('turn', 1, 0),
    ('first', 5),
    ('first', 12),
    ('first', 4),
    ('turn', 2, 1),
    ('leaf', 2),
    ('turn', 3, 1),
    ('first', 1),
    ('turn', 8, 0),
    ('leaf', 1),
    ('turn', 1, 1),
    ('turn', 6, 0),
    ('turn', 0, 2),
    ('turn', 8, 1),
    ('first', 8),
    ('turn', 4, 0),
    ('turn', 7, 0),
    ('turn', 2, 2),
    ('first', 10),
    ('turn', 7, 1),
    ('turn', 0, 3),
    ('turn', 5, 0),
    ('turn', 3, 2),
    ('first', 9),
    ('turn', 1, 2),
    ('turn', 11, 0),
    ('turn', 6, 1),
    ('turn', 2, 3),
    ('turn', 4, 1),
    ('turn', 7, 2),
    ('turn', 3, 3),
    ('turn', 10, 0),
    ('turn', 5, 1),
    ('turn', 8, 2),
    ('turn', 0, 4),
    ('turn', 6, 2),
    ('turn', 7, 3),
    ('turn', 1, 3),
    ('first', 7),
    ('turn', 9, 0),
    ('turn', 4, 2),
    ('turn', 8, 3),
    ('turn', 0, 5),
    ('turn', 11, 1),
    ('turn', 2, 4),
    ('turn', 1, 4),
    ('turn', 5, 2),
    ('turn', 8, 4),
    ('turn', 3, 4),
    ('turn', 6, 3),
    ('turn', 11, 2),
    ('turn', 9, 1),
    ('first', 2),
    ('first', 6),
    ('turn', 4, 3),
    ('turn', 5, 3),
    ('turn', 3, 5),
    ('turn', 10, 1),
    ('turn', 6, 4),
    ('turn', 2, 5),
    ('first', 13),
    ('turn', 1, 5),
    ('turn', 11, 3),
    ('turn', 9, 2),
    ('split', 1),
    ('first', 3),
    ('turn', 3, 6),
    ('turn', 6, 5),
    ('turn', 4, 4),
    ('turn', 8, 5),
    ('turn', 2, 6),
    ('turn', 10, 2),
    ('turn', 5, 4),
    ('first', 11),
    ('turn', 0, 6),
    ('turn', 4, 5),
    ('turn', 3, 7),
    ('turn', 1, 6),
    ('turn', 9, 3),
    ('turn', 2, 7),
    ('turn', 7, 4),
    ('turn', 8, 6),
    ('turn', 0, 7),
    ('turn', 3, 8),
    ('turn', 10, 3),
    ('turn', 5, 5),
    ('turn', 6, 6),
    ('turn', 9, 4),
    ('turn', 11, 4),
    ('split', 0),
    ('turn', 4, 6),
    ('turn', 0, 8),
    ('turn', 1, 7),
    ('split', 2),
    ('turn', 2, 8),
    ('turn', 7, 5),
    ('split', 3),
    ('contract', 2),
    ('turn', 10, 4),
    ('turn', 1, 8),
    ('turn', 5, 6),
    ('second', 14),
    ('turn', 11, 5),
    ('second', 10),
    ('contract', 0),
    ('contract', 3),
    ('turn', 10, 5),
    ('second', 12),
    ('second', 8),
    ('turn', 7, 6),
    ('contract', 1),
    ('turn', 11, 6),
    ('turn', 9, 5),
    ('turn', 10, 6),
    ('turn', 6, 7),
    ('turn', 7, 7),
    ('turn', 8, 7),
    ('second', 6),
    ('turn', 9, 6),
    ('second', 13),
    ('second', 5),
    ('turn', 4, 7),
    ('second', 11),
    ('turn', 5, 7),
    ('second', 15),
    ('turn', 4, 8),
    ('turn', 8, 8),
    ('turn', 7, 8),
    ('second', 4),
    ('turn', 11, 7),
    ('turn', 10, 7),
    ('second', 7),
    ('second', 1),
    ('turn', 11, 8),
    ('second', 2),
    ('second', 9),
    ('turn', 9, 7),
    ('turn', 10, 8),
    ('second', 3),
    ('turn', 6, 8),
    ('turn', 5, 8),
    ('multiply',),
    ('turn', 9, 8),
    ('absorb', 0),
    ('interleave',),
    ('absorb', 2),
    ('absorb', 3),
    ('absorb', 1),
]


def pieces_of(planes, span):
    parts = []
    for plane in range(planes):
        pieces = PIECES[plane // 2] if span % 32 == 0 else 1
        parts += [(plane, pl.ds(h * (span // pieces), span // pieces)) for h in range(pieces)]
    return parts


def schedule(n, steps, parts):
    if n == 16:
        return TABLE
    events = []

    def at(time, *event):
        events.append((time, event))

    stages = [STAGES[min(s, 3)] for s in range(steps)]
    stages = stages + stages[::-1]
    done = {}
    for c, (plane, _) in enumerate(parts):
        begin = ENTRIES[plane // 2] + GAP * (plane % 2)
        for step in range(2 * steps + 1):
            done[c, step] = begin + sum(stages[:step])
            at(done[c, step], "turn", c, step)
    chunks_of = [[c for c, (plane, _) in enumerate(parts) if plane // 2 == j] for j in range(4)]
    for j in LEAF_ORDER:
        at(ENTRIES[j] - 1, "leaf", j)
    ready = max(done[c, 2 * steps - 2] for c in chunks_of[0])
    for k in range(1, n):
        at(ready * k / (2 * n), "first", k)
    for i in range(4):
        at(ready * (i + 5) / 10, "split", i)
    for low, s in ((0, 2), (2, 1), (1, 0), (3, 0)):
        time = max(done[c, 2 * steps - s] for c in chunks_of[0]) + 0.01 * (1 + low)
        at(time, "contract", low)
        for q in range(n // 4):
            if q or low:
                at(time, "second", 4 * q + low)
    end = max(done.values()) + 1
    at(end, "interleave")
    at(end, "multiply")
    for i, low in enumerate((0, 2, 1, 3)):
        at(end + i + 1, "absorb", low)
    return [event for _, event in sorted(events, key=lambda entry: entry[0])]


def network_kernel(
    n, bits_in, stem, left, right, mixed_out, absorbed_out,
    bits,    l0, l1, l2, l3, l4, r0, r1, r2, r3, r4, part, outgoing, incoming, branch, got0, planes, blocks1, got1, absorbed,
    q_product, mixed, wide, leaf_sem, own_sem, a_send, a_recv, r_send, r_recv,
):
    planes_in, _, span, columns = part.shape
    parts = pieces_of(planes_in, span)
    chunks = len(parts)
    width = n * span
    steps = n.bit_length() - 1
    group = n // 4
    me = lax.axis_index("outer")
    lefts, rights = (l0, l1, l2, l3, l4), (r0, r1, r2, r3, r4)

    bit = [lax.rem(me // (1 << s), 2) for s in range(steps)]

    def flipped(k):
        return sum((1 - bit[s] if k >> s & 1 else bit[s]) * (1 << s) for s in range(steps))

    def reversed_bits(k):
        return sum(lax.rem(k // (1 << s), 2) * (n >> (s + 1)) for s in range(steps))

    partners = [me + (1 << s) * (1 - 2 * bit[s]) for s in range(steps)]
    starts = [0]
    gives = []
    for s in range(steps):
        half = n >> (s + 1)
        gives.append(starts[s] + (1 - bit[s]) * half)
        starts.append(starts[s] + bit[s] * half)

    barrier = pltpu.get_barrier_semaphore()

    def greet(k, carry):
        pl.semaphore_signal(barrier, inc=1, device_id={"outer": lax.rem(me + k, n)}, device_id_type=MESH)
        return carry

    lax.fori_loop(1, n, greet, 0)
    bits_copy = pltpu.make_async_copy(bits_in, bits, own_sem)
    bits_copy.start()

    depth = l1.shape[1]

    def leaf_copies(j, piece=0, pieces=1):
        here = pl.ds(piece * (depth // pieces), depth // pieces)
        return (
            pltpu.make_async_copy(left.at[j, :, here], lefts[j + 4 * piece], leaf_sem.at[j + 4 * piece, 0]),
            pltpu.make_async_copy(right.at[j, :, here], rights[j + 4 * piece], leaf_sem.at[j + 4 * piece, 1]),
        )

    def first_copy(k):
        to = flipped(k)
        return pltpu.make_async_remote_copy(
            src_ref=stem.at[to], dst_ref=got0.at[me], send_sem=a_send.at[k], recv_sem=a_recv.at[0, k // group],
            device_id={"outer": to}, device_id_type=MESH)

    def second_copy(k):
        to = flipped(k)
        return pltpu.make_async_remote_copy(
            src_ref=blocks1.at[reversed_bits(to)], dst_ref=got1.at[me // 4, lax.rem(me, 4)],
            send_sem=a_send.at[k], recv_sem=a_recv.at[1, k % 4],
            device_id={"outer": to}, device_id_type=MESH)

    own_copy = pltpu.make_async_copy(stem.at[me], got0.at[me], a_recv.at[0, 0])

    unsettled = {}

    def launch(copy, *slot):
        if slot in unsettled:
            unsettled[slot].wait_send()
        copy.start()
        unsettled[slot] = copy

    def send_first(k):
        launch(first_copy(k), k)

    def send_second(k):
        launch(second_copy(k), k)

    def split(i):
        here = pl.ds(flipped(group * i) // group * group, group)
        pltpu.make_async_copy(got0.at[here], got0.at[here], a_recv.at[0, i]).wait()
        rows = group * span
        entries = got0[here].reshape(2 * rows, columns).astype(jnp.float32)
        for t in range(columns // LANES):
            lanes = slice(t * LANES, (t + 1) * LANES)
            wide[t, 0 : 2 * rows] = entries[:, lanes]
            for p in range(2):
                plane = wide[t, pl.ds(p, rows, stride=2), :]
                planes[p, here, :, lanes] = plane.astype(jnp.bfloat16).reshape(group, span, LANES)

    def dot(a, b):
        return jnp.dot(a, b, preferred_element_type=jnp.float32)

    def leaf_product(j, piece=0, pieces=1):
        for copy in leaf_copies(j, piece, pieces):
            copy.wait()
        if j == 0 and piece == pieces - 1:
            for other in LEAF_ORDER:
                for copy in leaf_copies(other):
                    copy.start()
        chosen = bits[j]
        k = j + 4 * piece
        plain_ref, other_ref = (rights[k], lefts[k]) if j % 2 == 0 else (lefts[k], rights[k])
        rows = 2 * depth // pieces
        plain = plain_ref[chosen].reshape(rows, plain_ref.shape[3])
        other = other_ref[chosen].reshape(rows, other_ref.shape[3]).astype(jnp.float32)
        even = lax.rem(lax.broadcasted_iota(jnp.int32, other.shape, 0), 2) == 0
        signed = jnp.where(even, other, -other).astype(jnp.bfloat16)
        swapped = jnp.where(even, pltpu.roll(other, rows - 1, 0), pltpu.roll(other, 1, 0)).astype(jnp.bfloat16)
        dims = (((0,), (0,)), ((), ()))
        for p, factor in enumerate((signed, swapped)):
            product = lax.dot_general(plain, factor, dims, preferred_element_type=jnp.float32)
            product = product.reshape(n, span, columns)
            for b in range(n if j == 0 else 0):
                at = sum((b >> s & 1) * (n >> (s + 1)) for s in range(steps))
                if piece:
                    part[p, at] += product[b]
                else:
                    part[p, at] = product[b]
            if j:
                part[2 * j + p] = product

    def reduce_copy(c, s):
        half, at = n >> (s + 1), n - (n >> s)
        plane, rows = parts[c]
        return pltpu.make_async_remote_copy(
            src_ref=outgoing.at[plane, pl.ds(gives[s], half), rows], dst_ref=incoming.at[plane, pl.ds(at, half), rows],
            send_sem=r_send.at[c], recv_sem=r_recv.at[c, s],
            device_id={"outer": partners[s]}, device_id_type=MESH)

    def gather_copy(c, s, first):
        plane, rows = parts[c]
        here = branch.at[plane, pl.ds(first, n >> (s + 1)), rows]
        return pltpu.make_async_remote_copy(
            src_ref=here, dst_ref=here, send_sem=r_send.at[c], recv_sem=r_recv.at[c, 2 * steps - 1 - s],
            device_id={"outer": partners[s]}, device_id_type=MESH)

    def begin(c, step):
        if step < steps:
            plane, rows = parts[c]
            give = pl.ds(gives[step], n >> (step + 1))
            outgoing[plane, give, rows] = part[plane, give, rows].astype(outgoing.dtype)
            launch(reduce_copy(c, step), 'chunk', c)
        else:
            s = 2 * steps - 1 - step
            launch(gather_copy(c, s, starts[s + 1]), 'chunk', c)

    def finish(c, step):
        if step < steps:
            plane, rows = parts[c]
            half, at = n >> (step + 1), n - (n >> step)
            reduce_copy(c, step).wait_recv()
            keep = pl.ds(starts[step + 1], half)
            total = part[plane, keep, rows] + incoming[plane, pl.ds(at, half), rows].astype(jnp.float32)
            if step == steps - 1:
                branch[plane, keep, rows] = total.astype(branch.dtype)
            else:
                part[plane, keep, rows] = total
        else:
            s = 2 * steps - 1 - step
            gather_copy(c, s, gives[s]).wait_recv()

    def turn(c, step):
        if step:
            finish(c, step - 1)
        if step < 2 * steps:
            begin(c, step)

    def near(low):
        core = lax.rem(bit[0] + low % 2, 2)
        side = lax.rem(bit[1] + low // 2, 2)
        return core, side

    def contract_first(low):
        core, side = near(low)
        here = pl.ds(core * (n // 2) + side * (n // 4), group)
        p_real = branch[0, here].reshape(group * span, width)
        p_imag = branch[1, here].reshape(group * span, width)
        a_real, a_imag = planes[0].reshape(width, columns), planes[1].reshape(width, columns)
        real_part = (dot(p_real, a_real) - dot(p_imag, a_imag)).astype(jnp.bfloat16)
        imag_part = (dot(p_real, a_imag) + dot(p_imag, a_real)).astype(jnp.bfloat16)
        blocks1[here, 0:span] = real_part.reshape(group, span, columns)
        blocks1[here, span : 2 * span] = imag_part.reshape(group, span, columns)
        if low == 0:
            got1[me // 4, lax.rem(me, 4)] = blocks1[starts[steps]]

    stored = []

    def put(source, target, semaphore):
        copy = pltpu.make_async_copy(source, target, semaphore)
        copy.start()
        stored.append(copy)

    def interleave():
        for t in range(width // LANES):
            lanes = slice(t * LANES, (t + 1) * LANES)
            p_real, p_imag = (
                branch[4 + p, :, :, lanes].reshape(width, LANES).astype(jnp.float32) for p in range(2))
            for k, (even, odd) in enumerate(((p_real, p_imag), (-p_imag, p_real))):
                wide[t, pl.ds(0, width, stride=2), :] = even
                wide[t, pl.ds(1, width, stride=2), :] = odd
                mixed[k, :, lanes] = wide[t].astype(jnp.bfloat16)
        put(mixed, mixed_out, own_sem)

    def multiply():
        a_real, a_imag, b_real, b_imag = (branch[c].reshape(width, columns) for c in (2, 3, 6, 7))
        q_product[0] = (dot(a_real, b_real) - dot(a_imag, b_imag)).astype(jnp.bfloat16)
        q_product[1] = (dot(a_real, b_imag) + dot(a_imag, b_real)).astype(jnp.bfloat16)

    def absorb(low):
        fill = got1.at[pl.ds(0, group if low else group - 1), 0]
        pltpu.make_async_copy(fill, fill, a_recv.at[1, low]).wait()
        core, side = near(low)
        entries = got1[:, core + 2 * side].reshape(group * 2 * span, columns)
        by_real = dot(entries, q_product[0]).reshape(group, 2, span, columns)
        by_imag = dot(entries, q_product[1]).reshape(group, 2, span, columns)
        absorbed[0, :, core + 2 * side] = (by_real[:, 0] - by_imag[:, 1]).astype(absorbed.dtype)
        absorbed[1, :, core + 2 * side] = (by_imag[:, 0] + by_real[:, 1]).astype(absorbed.dtype)
        for p in range(2):
            put(absorbed.at[p, :, core + 2 * side], absorbed_out.at[p, :, core + 2 * side], leaf_sem.at[low, p])

    for piece in range(HALVES):
        for copy in leaf_copies(0, piece, HALVES):
            copy.start()
    own_copy.start()
    bits_copy.wait()
    for piece in range(HALVES):
        leaf_product(0, piece, HALVES)
    pl.semaphore_wait(barrier, n - 1)

    acts = dict(
        leaf=leaf_product, turn=turn, first=send_first, split=split, contract=contract_first, second=send_second,
        interleave=interleave, multiply=multiply, absorb=absorb)
    for name, *arguments in schedule(n, steps, parts):
        acts[name](*arguments)

    for copy in unsettled.values():
        copy.wait_send()
    for copy in stored:
        copy.wait()


def last_kernel(mixed, absorbed, out, mixed_here, absorbed_here, out_here, semaphores):
    rows = mixed.shape[1] // TILES
    copies = []
    for tile in range(TILES):
        here = pl.ds(tile * rows, rows)
        copies.append(pltpu.make_async_copy(mixed.at[:, here], mixed_here.at[:, here], semaphores.at[tile]))
    fetch = pltpu.make_async_copy(absorbed, absorbed_here, semaphores.at[TILES])
    copies[0].start()
    fetch.start()
    for copy in copies[1:]:
        copy.start()
    stores = []
    for tile, copy in enumerate(copies):
        copy.wait()
        if tile == 0:
            fetch.wait()
        here = pl.ds(tile * rows, rows)
        half = pl.ds(tile * (rows // 2), rows // 2)
        total = jnp.dot(mixed_here[0, here], absorbed_here[0], preferred_element_type=jnp.float32)
        total = total + jnp.dot(mixed_here[1, here], absorbed_here[1], preferred_element_type=jnp.float32)
        out_here[half] = total.astype(out.dtype).reshape(rows // 2, 2, out.shape[2])
        stores.append(pltpu.make_async_copy(out_here.at[half], out.at[half], semaphores.at[tile]))
        stores[-1].start()
    for store in stores:
        store.wait()


def contract_last(mixed, absorbed):
    _, rows, width = mixed.shape
    columns = absorbed.shape[2]
    anywhere = pl.BlockSpec(memory_space=pl.ANY)
    return pl.pallas_call(
        last_kernel,
        out_shape=jax.ShapeDtypeStruct((rows // 2, 2, columns), jnp.bfloat16),
        in_specs=[anywhere, anywhere],
        out_specs=anywhere,
        scratch_shapes=[
            pltpu.VMEM(mixed.shape, mixed.dtype),
            pltpu.VMEM(absorbed.shape, absorbed.dtype),
            pltpu.VMEM((rows // 2, 2, columns), jnp.bfloat16),
            pltpu.SemaphoreType.DMA((TILES + 1,)),
        ],
    )(mixed, absorbed)


def on_device(n, stem_tensor, leaf_left, leaf_right, slice_bits):
    branches, slices, depth, _, rows = leaf_left.shape
    width, columns = stem_tensor.shape[1], stem_tensor.shape[3]
    span = width // n
    steps = n.bit_length() - 1
    chunks = len(pieces_of(2 * branches, span))
    blocks = stem_tensor.reshape(n, span, 2, columns)
    both = (2 * branches, n, span, columns)
    anywhere = pl.BlockSpec(memory_space=pl.ANY)
    sizes = [depth // HALVES, *[depth] * (branches - 1), depth // HALVES]
    mixed, absorbed = pl.pallas_call(
        functools.partial(network_kernel, n),
        out_shape=(
            jax.ShapeDtypeStruct((2, 2 * width, width), jnp.bfloat16),
            jax.ShapeDtypeStruct((2, n // 4, 4, span, columns), jnp.bfloat16),
        ),
        in_specs=[anywhere, anywhere, anywhere, anywhere],
        out_specs=(anywhere, anywhere),
        scratch_shapes=[
            pltpu.SMEM((branches,), jnp.int32),
            *[pltpu.VMEM((slices, size, 2, rows), jnp.bfloat16) for size in sizes],
            *[pltpu.VMEM((slices, size, 2, columns), jnp.bfloat16) for size in sizes],
            pltpu.VMEM(both, jnp.float32),
            pltpu.VMEM(both, jnp.bfloat16),
            pltpu.VMEM(both, jnp.bfloat16),
            pltpu.VMEM(both, jnp.bfloat16),
            pltpu.VMEM((n, span, 2, columns), jnp.bfloat16),
            pltpu.VMEM((2, n, span, columns), jnp.bfloat16),
            pltpu.VMEM((n, 2 * span, columns), jnp.bfloat16),
            pltpu.VMEM((n // 4, 4, 2 * span, columns), jnp.bfloat16),
            pltpu.VMEM((2, n // 4, 4, span, columns), jnp.bfloat16),
            pltpu.VMEM((2, width, columns), jnp.bfloat16),
            pltpu.VMEM((2, 2 * width, columns), jnp.bfloat16),
            pltpu.VMEM((columns // LANES, 2 * width, LANES), jnp.float32),
            pltpu.SemaphoreType.DMA((branches + 1, 2)),
            pltpu.SemaphoreType.DMA,
            pltpu.SemaphoreType.DMA((n,)),
            pltpu.SemaphoreType.DMA((2, 4)),
            pltpu.SemaphoreType.DMA((chunks,)),
            pltpu.SemaphoreType.DMA((chunks, 2 * steps)),
        ],
        compiler_params=pltpu.CompilerParams(
            collective_id=0, has_side_effects=True, vmem_limit_bytes=60 * 1024 * 1024),
    )(slice_bits, blocks, leaf_left, leaf_right)
    return contract_last(mixed, absorbed.reshape(2, width, columns))[None]


def solution(mesh):
    return jax.shard_map(
        functools.partial(on_device, mesh.shape["outer"]),
        mesh=mesh,
        in_specs=(
            P(("cuts", "outer"), None, None, None),
            P(None, None, "outer", None, None),
            P(None, None, "outer", None, None),
            P("cuts"),
        ),
        out_specs=P(("cuts", "outer"), None, None, None),
        check_vma=False,
    )
```

```python
import functools

import jax
import jax.numpy as jnp
from jax import lax
from jax.experimental import pallas as pl
from jax.experimental.pallas import tpu as pltpu
from jax.sharding import PartitionSpec as P

MESH = pl.DeviceIdType.MESH
LANES = 128
TILES = 4
HALVES = 2
LEAF_ORDER = (3, 2, 1)
PIECES = (2, 1, 2, 1)


STAGES = (1.6, 4.5, 3.5, 3.5)
ENTRIES = (0.5, 15.0, 7.0, 20.0)
GAP = 0.4
TABLE = [
    ('first', 15),
    ('first', 14),
    ('turn', 0, 0),
    ('turn', 3, 0),
    ('turn', 1, 0),
    ('leaf', 3),
    ('turn', 2, 0),
    ('turn', 0, 1),
    ('first', 5),
    ('first', 12),
    ('first', 4),
    ('turn', 2, 1),
    ('leaf', 2),
    ('turn', 3, 1),
    ('first', 1),
    ('turn', 8, 0),
    ('leaf', 1),
    ('turn', 1, 1),
    ('turn', 6, 0),
    ('turn', 0, 2),
    ('turn', 8, 1),
    ('first', 8),
    ('turn', 4, 0),
    ('turn', 7, 0),
    ('turn', 2, 2),
    ('first', 10),
    ('turn', 7, 1),
    ('turn', 0, 3),
    ('turn', 5, 0),
    ('turn', 3, 2),
    ('first', 9),
    ('turn', 1, 2),
    ('turn', 11, 0),
    ('turn', 6, 1),
    ('turn', 2, 3),
    ('turn', 4, 1),
    ('turn', 7, 2),
    ('turn', 3, 3),
    ('first', 6),
    ('turn', 10, 0),
    ('turn', 5, 1),
    ('turn', 8, 2),
    ('turn', 0, 4),
    ('turn', 6, 2),
    ('turn', 7, 3),
    ('turn', 1, 3),
    ('first', 7),
    ('turn', 9, 0),
    ('turn', 4, 2),
    ('turn', 8, 3),
    ('turn', 0, 5),
    ('turn', 11, 1),
    ('turn', 2, 4),
    ('turn', 1, 4),
    ('turn', 5, 2),
    ('turn', 8, 4),
    ('turn', 3, 4),
    ('turn', 6, 3),
    ('turn', 11, 2),
    ('turn', 9, 1),
    ('first', 2),
    ('turn', 4, 3),
    ('turn', 5, 3),
    ('turn', 3, 5),
    ('turn', 6, 4),
    ('turn', 10, 1),
    ('turn', 2, 5),
    ('first', 13),
    ('turn', 1, 5),
    ('turn', 11, 3),
    ('turn', 9, 2),
    ('split', 1),
    ('first', 3),
    ('turn', 3, 6),
    ('turn', 6, 5),
    ('turn', 4, 4),
    ('turn', 8, 5),
    ('turn', 2, 6),
    ('turn', 5, 4),
    ('turn', 10, 2),
    ('first', 11),
    ('turn', 0, 6),
    ('turn', 4, 5),
    ('turn', 3, 7),
    ('turn', 1, 6),
    ('turn', 9, 3),
    ('turn', 2, 7),
    ('turn', 7, 4),
    ('turn', 8, 6),
    ('turn', 0, 7),
    ('turn', 3, 8),
    ('turn', 10, 3),
    ('turn', 5, 5),
    ('turn', 6, 6),
    ('turn', 9, 4),
    ('turn', 11, 4),
    ('split', 0),
    ('turn', 4, 6),
    ('turn', 0, 8),
    ('turn', 1, 7),
    ('split', 2),
    ('turn', 7, 5),
    ('turn', 2, 8),
    ('split', 3),
    ('contract', 2),
    ('turn', 10, 4),
    ('turn', 1, 8),
    ('turn', 5, 6),
    ('second', 14),
    ('turn', 11, 5),
    ('second', 10),
    ('contract', 0),
    ('contract', 3),
    ('turn', 10, 5),
    ('second', 12),
    ('second', 8),
    ('turn', 7, 6),
    ('turn', 11, 6),
    ('turn', 9, 5),
    ('turn', 10, 6),
    ('turn', 6, 7),
    ('contract', 1),
    ('turn', 7, 7),
    ('turn', 8, 7),
    ('second', 6),
    ('turn', 9, 6),
    ('second', 13),
    ('second', 5),
    ('turn', 4, 7),
    ('second', 11),
    ('turn', 5, 7),
    ('second', 15),
    ('turn', 4, 8),
    ('turn', 8, 8),
    ('turn', 7, 8),
    ('second', 4),
    ('turn', 11, 7),
    ('turn', 10, 7),
    ('second', 7),
    ('second', 1),
    ('second', 2),
    ('second', 9),
    ('turn', 9, 7),
    ('turn', 10, 8),
    ('second', 3),
    ('turn', 11, 8),
    ('turn', 6, 8),
    ('turn', 5, 8),
    ('multiply',),
    ('turn', 9, 8),
    ('absorb', 0),
    ('interleave',),
    ('absorb', 2),
    ('absorb', 3),
    ('absorb', 1),
]


def pieces_of(planes, span):
    parts = []
    for plane in range(planes):
        pieces = PIECES[plane // 2] if span % 32 == 0 else 1
        parts += [(plane, pl.ds(h * (span // pieces), span // pieces)) for h in range(pieces)]
    return parts


def schedule(n, steps, parts):
    if n == 16:
        return TABLE
    events = []

    def at(time, *event):
        events.append((time, event))

    stages = [STAGES[min(s, 3)] for s in range(steps)]
    stages = stages + stages[::-1]
    done = {}
    for c, (plane, _) in enumerate(parts):
        begin = ENTRIES[plane // 2] + GAP * (plane % 2)
        for step in range(2 * steps + 1):
            done[c, step] = begin + sum(stages[:step])
            at(done[c, step], "turn", c, step)
    chunks_of = [[c for c, (plane, _) in enumerate(parts) if plane // 2 == j] for j in range(4)]
    for j in LEAF_ORDER:
        at(ENTRIES[j] - 1, "leaf", j)
    ready = max(done[c, 2 * steps - 2] for c in chunks_of[0])
    for k in range(1, n):
        at(ready * k / (2 * n), "first", k)
    for i in range(4):
        at(ready * (i + 5) / 10, "split", i)
    for low, s in ((0, 2), (2, 1), (1, 0), (3, 0)):
        time = max(done[c, 2 * steps - s] for c in chunks_of[0]) + 0.01 * (1 + low)
        at(time, "contract", low)
        for q in range(n // 4):
            if q or low:
                at(time, "second", 4 * q + low)
    end = max(done.values()) + 1
    at(end, "interleave")
    at(end, "multiply")
    for i, low in enumerate((0, 2, 1, 3)):
        at(end + i + 1, "absorb", low)
    return [event for _, event in sorted(events, key=lambda entry: entry[0])]


def network_kernel(
    n, bits_in, stem, left, right, mixed_out, absorbed_out,
    bits,    l0, l1, l2, l3, l4, r0, r1, r2, r3, r4, part, outgoing, incoming, branch, got0, planes, blocks1, got1, absorbed,
    q_product, mixed, wide, leaf_sem, own_sem, a_send, a_recv, r_send, r_recv,
):
    planes_in, _, span, columns = part.shape
    parts = pieces_of(planes_in, span)
    chunks = len(parts)
    width = n * span
    steps = n.bit_length() - 1
    group = n // 4
    me = lax.axis_index("outer")
    lefts, rights = (l0, l1, l2, l3, l4), (r0, r1, r2, r3, r4)

    bit = [lax.rem(me // (1 << s), 2) for s in range(steps)]

    def flipped(k):
        return sum((1 - bit[s] if k >> s & 1 else bit[s]) * (1 << s) for s in range(steps))

    def reversed_bits(k):
        return sum(lax.rem(k // (1 << s), 2) * (n >> (s + 1)) for s in range(steps))

    partners = [me + (1 << s) * (1 - 2 * bit[s]) for s in range(steps)]
    starts = [0]
    gives = []
    for s in range(steps):
        half = n >> (s + 1)
        gives.append(starts[s] + (1 - bit[s]) * half)
        starts.append(starts[s] + bit[s] * half)

    barrier = pltpu.get_barrier_semaphore()

    def greet(k, carry):
        pl.semaphore_signal(barrier, inc=1, device_id={"outer": lax.rem(me + k, n)}, device_id_type=MESH)
        return carry

    lax.fori_loop(1, n, greet, 0)
    bits_copy = pltpu.make_async_copy(bits_in, bits, own_sem)
    bits_copy.start()

    depth = l1.shape[1]

    def leaf_copies(j, piece=0, pieces=1):
        here = pl.ds(piece * (depth // pieces), depth // pieces)
        return (
            pltpu.make_async_copy(left.at[j, :, here], lefts[j + 4 * piece], leaf_sem.at[j + 4 * piece, 0]),
            pltpu.make_async_copy(right.at[j, :, here], rights[j + 4 * piece], leaf_sem.at[j + 4 * piece, 1]),
        )

    def first_copy(k):
        to = flipped(k)
        return pltpu.make_async_remote_copy(
            src_ref=stem.at[to], dst_ref=got0.at[me], send_sem=a_send.at[k], recv_sem=a_recv.at[0, k // group],
            device_id={"outer": to}, device_id_type=MESH)

    def second_copy(k):
        to = flipped(k)
        return pltpu.make_async_remote_copy(
            src_ref=blocks1.at[reversed_bits(to)], dst_ref=got1.at[me // 4, lax.rem(me, 4)],
            send_sem=a_send.at[k], recv_sem=a_recv.at[1, k % 4],
            device_id={"outer": to}, device_id_type=MESH)

    own_copy = pltpu.make_async_copy(stem.at[me], got0.at[me], a_recv.at[0, 0])

    unsettled = {}

    def launch(copy, *slot):
        if slot in unsettled:
            unsettled[slot].wait_send()
        copy.start()
        unsettled[slot] = copy

    def send_first(k):
        launch(first_copy(k), k)

    def send_second(k):
        launch(second_copy(k), k)

    def split(i):
        here = pl.ds(flipped(group * i) // group * group, group)
        pltpu.make_async_copy(got0.at[here], got0.at[here], a_recv.at[0, i]).wait()
        rows = group * span
        entries = got0[here].reshape(2 * rows, columns).astype(jnp.float32)
        for t in range(columns // LANES):
            lanes = slice(t * LANES, (t + 1) * LANES)
            wide[t, 0 : 2 * rows] = entries[:, lanes]
            for p in range(2):
                plane = wide[t, pl.ds(p, rows, stride=2), :]
                planes[p, here, :, lanes] = plane.astype(jnp.bfloat16).reshape(group, span, LANES)

    def dot(a, b):
        return jnp.dot(a, b, preferred_element_type=jnp.float32)

    def leaf_product(j, piece=0, pieces=1):
        for copy in leaf_copies(j, piece, pieces):
            copy.wait()
        if j == 0 and piece == pieces - 1:
            for other in LEAF_ORDER:
                for copy in leaf_copies(other):
                    copy.start()
        chosen = bits[j]
        k = j + 4 * piece
        plain_ref, other_ref = (rights[k], lefts[k]) if j % 2 == 0 else (lefts[k], rights[k])
        rows = 2 * depth // pieces
        plain = plain_ref[chosen].reshape(rows, plain_ref.shape[3])
        other = other_ref[chosen].reshape(rows, other_ref.shape[3]).astype(jnp.float32)
        even = lax.rem(lax.broadcasted_iota(jnp.int32, other.shape, 0), 2) == 0
        signed = jnp.where(even, other, -other).astype(jnp.bfloat16)
        swapped = jnp.where(even, pltpu.roll(other, rows - 1, 0), pltpu.roll(other, 1, 0)).astype(jnp.bfloat16)
        dims = (((0,), (0,)), ((), ()))
        for p, factor in enumerate((signed, swapped)):
            product = lax.dot_general(plain, factor, dims, preferred_element_type=jnp.float32)
            product = product.reshape(n, span, columns)
            for b in range(n if j == 0 else 0):
                at = sum((b >> s & 1) * (n >> (s + 1)) for s in range(steps))
                if piece:
                    part[p, at] += product[b]
                else:
                    part[p, at] = product[b]
            if j:
                part[2 * j + p] = product

    def reduce_copy(c, s):
        half, at = n >> (s + 1), n - (n >> s)
        plane, rows = parts[c]
        return pltpu.make_async_remote_copy(
            src_ref=outgoing.at[plane, pl.ds(gives[s], half), rows], dst_ref=incoming.at[plane, pl.ds(at, half), rows],
            send_sem=r_send.at[c], recv_sem=r_recv.at[c, s],
            device_id={"outer": partners[s]}, device_id_type=MESH)

    def gather_copy(c, s, first):
        plane, rows = parts[c]
        here = branch.at[plane, pl.ds(first, n >> (s + 1)), rows]
        return pltpu.make_async_remote_copy(
            src_ref=here, dst_ref=here, send_sem=r_send.at[c], recv_sem=r_recv.at[c, 2 * steps - 1 - s],
            device_id={"outer": partners[s]}, device_id_type=MESH)

    def begin(c, step):
        if step < steps:
            plane, rows = parts[c]
            give = pl.ds(gives[step], n >> (step + 1))
            outgoing[plane, give, rows] = part[plane, give, rows].astype(outgoing.dtype)
            launch(reduce_copy(c, step), 'chunk', c)
        else:
            s = 2 * steps - 1 - step
            launch(gather_copy(c, s, starts[s + 1]), 'chunk', c)

    def finish(c, step):
        if step < steps:
            plane, rows = parts[c]
            half, at = n >> (step + 1), n - (n >> step)
            reduce_copy(c, step).wait_recv()
            keep = pl.ds(starts[step + 1], half)
            total = part[plane, keep, rows] + incoming[plane, pl.ds(at, half), rows].astype(jnp.float32)
            if step == steps - 1:
                branch[plane, keep, rows] = total.astype(branch.dtype)
            else:
                part[plane, keep, rows] = total
        else:
            s = 2 * steps - 1 - step
            gather_copy(c, s, gives[s]).wait_recv()

    def turn(c, step):
        if step:
            finish(c, step - 1)
        if step < 2 * steps:
            begin(c, step)

    def near(low):
        core = lax.rem(bit[0] + low % 2, 2)
        side = lax.rem(bit[1] + low // 2, 2)
        return core, side

    def contract_first(low):
        core, side = near(low)
        here = pl.ds(core * (n // 2) + side * (n // 4), group)
        p_real = branch[0, here].reshape(group * span, width)
        p_imag = branch[1, here].reshape(group * span, width)
        a_real, a_imag = planes[0].reshape(width, columns), planes[1].reshape(width, columns)
        real_part = (dot(p_real, a_real) - dot(p_imag, a_imag)).astype(jnp.bfloat16)
        imag_part = (dot(p_real, a_imag) + dot(p_imag, a_real)).astype(jnp.bfloat16)
        blocks1[here, 0:span] = real_part.reshape(group, span, columns)
        blocks1[here, span : 2 * span] = imag_part.reshape(group, span, columns)
        if low == 0:
            got1[me // 4, lax.rem(me, 4)] = blocks1[starts[steps]]

    stored = []

    def put(source, target, semaphore):
        copy = pltpu.make_async_copy(source, target, semaphore)
        copy.start()
        stored.append(copy)

    def interleave():
        for t in range(width // LANES):
            lanes = slice(t * LANES, (t + 1) * LANES)
            p_real, p_imag = (
                branch[4 + p, :, :, lanes].reshape(width, LANES).astype(jnp.float32) for p in range(2))
            for k, (even, odd) in enumerate(((p_real, p_imag), (-p_imag, p_real))):
                wide[t, pl.ds(0, width, stride=2), :] = even
                wide[t, pl.ds(1, width, stride=2), :] = odd
                mixed[k, :, lanes] = wide[t].astype(jnp.bfloat16)
        put(mixed, mixed_out, own_sem)

    def multiply():
        a_real, a_imag, b_real, b_imag = (branch[c].reshape(width, columns) for c in (2, 3, 6, 7))
        q_product[0] = (dot(a_real, b_real) - dot(a_imag, b_imag)).astype(jnp.bfloat16)
        q_product[1] = (dot(a_real, b_imag) + dot(a_imag, b_real)).astype(jnp.bfloat16)

    def absorb(low):
        fill = got1.at[pl.ds(0, group if low else group - 1), 0]
        pltpu.make_async_copy(fill, fill, a_recv.at[1, low]).wait()
        core, side = near(low)
        entries = got1[:, core + 2 * side].reshape(group * 2 * span, columns)
        by_real = dot(entries, q_product[0]).reshape(group, 2, span, columns)
        by_imag = dot(entries, q_product[1]).reshape(group, 2, span, columns)
        absorbed[0, :, core + 2 * side] = (by_real[:, 0] - by_imag[:, 1]).astype(absorbed.dtype)
        absorbed[1, :, core + 2 * side] = (by_imag[:, 0] + by_real[:, 1]).astype(absorbed.dtype)
        for p in range(2):
            put(absorbed.at[p, :, core + 2 * side], absorbed_out.at[p, :, core + 2 * side], leaf_sem.at[low, p])

    for piece in range(HALVES):
        for copy in leaf_copies(0, piece, HALVES):
            copy.start()
    own_copy.start()
    bits_copy.wait()
    for piece in range(HALVES):
        leaf_product(0, piece, HALVES)
    pl.semaphore_wait(barrier, n - 1)

    acts = dict(
        leaf=leaf_product, turn=turn, first=send_first, split=split, contract=contract_first, second=send_second,
        interleave=interleave, multiply=multiply, absorb=absorb)
    for name, *arguments in schedule(n, steps, parts):
        acts[name](*arguments)

    for copy in unsettled.values():
        copy.wait_send()
    for copy in stored:
        copy.wait()


def last_kernel(mixed, absorbed, out, mixed_here, absorbed_here, out_here, semaphores):
    rows = mixed.shape[1] // TILES
    copies = []
    for tile in range(TILES):
        here = pl.ds(tile * rows, rows)
        copies.append(pltpu.make_async_copy(mixed.at[:, here], mixed_here.at[:, here], semaphores.at[tile]))
    fetch = pltpu.make_async_copy(absorbed, absorbed_here, semaphores.at[TILES])
    copies[0].start()
    fetch.start()
    for copy in copies[1:]:
        copy.start()
    stores = []
    for tile, copy in enumerate(copies):
        copy.wait()
        if tile == 0:
            fetch.wait()
        here = pl.ds(tile * rows, rows)
        half = pl.ds(tile * (rows // 2), rows // 2)
        total = jnp.dot(mixed_here[0, here], absorbed_here[0], preferred_element_type=jnp.float32)
        total = total + jnp.dot(mixed_here[1, here], absorbed_here[1], preferred_element_type=jnp.float32)
        out_here[half] = total.astype(out.dtype).reshape(rows // 2, 2, out.shape[2])
        stores.append(pltpu.make_async_copy(out_here.at[half], out.at[half], semaphores.at[tile]))
        stores[-1].start()
    for store in stores:
        store.wait()


def contract_last(mixed, absorbed):
    _, rows, width = mixed.shape
    columns = absorbed.shape[2]
    anywhere = pl.BlockSpec(memory_space=pl.ANY)
    return pl.pallas_call(
        last_kernel,
        out_shape=jax.ShapeDtypeStruct((rows // 2, 2, columns), jnp.bfloat16),
        in_specs=[anywhere, anywhere],
        out_specs=anywhere,
        scratch_shapes=[
            pltpu.VMEM(mixed.shape, mixed.dtype),
            pltpu.VMEM(absorbed.shape, absorbed.dtype),
            pltpu.VMEM((rows // 2, 2, columns), jnp.bfloat16),
            pltpu.SemaphoreType.DMA((TILES + 1,)),
        ],
    )(mixed, absorbed)


def on_device(n, stem_tensor, leaf_left, leaf_right, slice_bits):
    branches, slices, depth, _, rows = leaf_left.shape
    width, columns = stem_tensor.shape[1], stem_tensor.shape[3]
    span = width // n
    steps = n.bit_length() - 1
    chunks = len(pieces_of(2 * branches, span))
    blocks = stem_tensor.reshape(n, span, 2, columns)
    both = (2 * branches, n, span, columns)
    anywhere = pl.BlockSpec(memory_space=pl.ANY)
    sizes = [depth // HALVES, *[depth] * (branches - 1), depth // HALVES]
    mixed, absorbed = pl.pallas_call(
        functools.partial(network_kernel, n),
        out_shape=(
            jax.ShapeDtypeStruct((2, 2 * width, width), jnp.bfloat16),
            jax.ShapeDtypeStruct((2, n // 4, 4, span, columns), jnp.bfloat16),
        ),
        in_specs=[anywhere, anywhere, anywhere, anywhere],
        out_specs=(anywhere, anywhere),
        scratch_shapes=[
            pltpu.SMEM((branches,), jnp.int32),
            *[pltpu.VMEM((slices, size, 2, rows), jnp.bfloat16) for size in sizes],
            *[pltpu.VMEM((slices, size, 2, columns), jnp.bfloat16) for size in sizes],
            pltpu.VMEM(both, jnp.float32),
            pltpu.VMEM(both, jnp.bfloat16),
            pltpu.VMEM(both, jnp.bfloat16),
            pltpu.VMEM(both, jnp.bfloat16),
            pltpu.VMEM((n, span, 2, columns), jnp.bfloat16),
            pltpu.VMEM((2, n, span, columns), jnp.bfloat16),
            pltpu.VMEM((n, 2 * span, columns), jnp.bfloat16),
            pltpu.VMEM((n // 4, 4, 2 * span, columns), jnp.bfloat16),
            pltpu.VMEM((2, n // 4, 4, span, columns), jnp.bfloat16),
            pltpu.VMEM((2, width, columns), jnp.bfloat16),
            pltpu.VMEM((2, 2 * width, columns), jnp.bfloat16),
            pltpu.VMEM((columns // LANES, 2 * width, LANES), jnp.float32),
            pltpu.SemaphoreType.DMA((branches + 1, 2)),
            pltpu.SemaphoreType.DMA,
            pltpu.SemaphoreType.DMA((n,)),
            pltpu.SemaphoreType.DMA((2, 4)),
            pltpu.SemaphoreType.DMA((chunks,)),
            pltpu.SemaphoreType.DMA((chunks, 2 * steps)),
        ],
        compiler_params=pltpu.CompilerParams(
            collective_id=0, has_side_effects=True, vmem_limit_bytes=60 * 1024 * 1024),
    )(slice_bits, blocks, leaf_left, leaf_right)
    return contract_last(mixed, absorbed.reshape(2, width, columns))[None]


def solution(mesh):
    return jax.shard_map(
        functools.partial(on_device, mesh.shape["outer"]),
        mesh=mesh,
        in_specs=(
            P(("cuts", "outer"), None, None, None),
            P(None, None, "outer", None, None),
            P(None, None, "outer", None, None),
            P("cuts"),
        ),
        out_specs=P(("cuts", "outer"), None, None, None),
        check_vma=False,
    )
```
